256 devices in a mesh: ctx: 16 (over y, x), exp: 8 (over z), dp: 2 (over core).
Axes of the slice: x: 4, y: 4, z: 8, core: 2. Of those that a mesh axis runs over, the one named last changes fastest.
Arguments:
- residual: bfloat16 [2048, 4096], P('ctx', ('exp', 'dp')), may hold values from -6 to 6
- ssm_values: bfloat16 [2048, 4096], P('ctx', ('exp', 'dp')), may hold values from -6 to 6
- ssm_keys: bfloat16 [2048, 64], P('ctx'), may hold values from -6 to 6
- ssm_queries: bfloat16 [2048, 64], P('ctx'), may hold values from -0.015625 to 0.015625
- log_decay: float32 [2048, 64], P('ctx', ('exp', 'dp')), may hold values from -1 to 0, as said below
- expert_ids: int32 [2048, 2], P('ctx'), may hold values from 0 to 7, all different within a row; in each aligned block of 128 rows (0 to 127, 128 to 255, ...) at most 40 rows name the same one
- gate_probs: float32 [2048, 2], P('ctx'), may hold values from 0.2 to 1
- norm_gain: float32 [4096], P(('exp', 'dp')), may hold values from 0.5 to 1.5
- w_gate: bfloat16 [8, 4096, 8192], P('exp', None, ('ctx', 'dp')), may hold values from -0.09375 to 0.09375
- w_up: bfloat16 [8, 4096, 8192], P('exp', None, ('ctx', 'dp')), may hold values from -0.09375 to 0.09375
- w_down: bfloat16 [8, 4096, 8192], P('exp', None, ('ctx', 'dp')), may hold values from -0.0625 to 0.0625
- out_grad: bfloat16 [2048, 4096], P('ctx', ('exp', 'dp')), may hold values from -6 to 6
Outputs:
- grad_residual: bfloat16 [2048, 4096], P('ctx', ('exp', 'dp'))
- grad_values: bfloat16 [2048, 4096], P('ctx', ('exp', 'dp'))
- grad_keys: float32 [2048, 64], P('ctx')
- grad_queries: float32 [2048, 64], P('ctx')
- grad_decay: float32 [2048, 64], P('ctx', ('exp', 'dp'))
- grad_probs: float32 [2048, 2], P('ctx')
- grad_gain: float32 [4096], P(('exp', 'dp'))
- w_gate_grad: bfloat16 [8, 4096, 8192], P('exp', None, ('ctx', 'dp'))
- w_up_grad: bfloat16 [8, 4096, 8192], P('exp', None, ('ctx', 'dp'))
- w_down_grad: bfloat16 [8, 4096, 8192], P('exp', None, ('ctx', 'dp'))
The draws below stay inside these ranges and needn't reach their ends.
Inputs may be any that keep to these rules, and one draw needn't show every extreme that they name: `expert_ids`: each token names two different experts; among the 128 tokens of one index of ctx (aligned blocks) no expert is named more than 40 times, a bound that some block reaches. `log_decay`: negative everywhere.
All inputs are finite; a program needn't handle non-finite values.
Results may differ from the reference program's by a relative error of at most 0.028.
Values may be sent and summed in bfloat16 or wider, within the bound.
No kernel may reach another device: no remote copies, remote signals or barrier semaphores. Data moves between devices by JAX's collectives and lax.ppermute only.
A program may use at most 128 MiB of HBM per device.

```python
import math
import jax
import jax.numpy as jnp
import numpy as np
from jax import lax

D = 4096
HEADS = 64
HDIM = 64
STATE = 64
FW = 8192
TOK_DEV = 128
EXPERTS = 8
FW_DEV = 256
SEQUENCE_LENGTH = 2048
CAP = 40
N_CTX = 16


def draw_log_decay(key, part):
    random_subkeys = jax.random.split(key, 7)
    complete_shape = (SEQUENCE_LENGTH, HEADS)
    fast_share = 0.4
    fast_mask = (jax.random.uniform(random_subkeys[0], (1, HEADS)) < fast_share).astype(jnp.float32)
    fast_rate = jnp.exp(jax.random.uniform(random_subkeys[1], (1, HEADS), minval=math.log(1.0 / 50.0), maxval=math.log(1.0 / 30.0)))
    slow_rate = jax.random.uniform(random_subkeys[2], (1, HEADS), minval=0.1, maxval=0.4) * (math.log(10.0) / SEQUENCE_LENGTH)
    baseline_decay_rate = fast_mask * fast_rate + (1.0 - fast_mask) * slow_rate
    blocks = SEQUENCE_LENGTH // TOK_DEV
    block_scale_factor = jnp.exp(jax.random.uniform(random_subkeys[3], (blocks, 1, HEADS), minval=math.log(0.5), maxval=math.log(2.0)))
    block_scale_factor = jnp.broadcast_to(block_scale_factor, (blocks, TOK_DEV, HEADS)).reshape(complete_shape)
    random_noise = jax.random.uniform(random_subkeys[4], complete_shape, minval=0.7, maxval=1.4)
    spike_position = jax.random.randint(random_subkeys[5], (1, 2), 0, SEQUENCE_LENGTH)
    sequence_position = jnp.arange(SEQUENCE_LENGTH, dtype=jnp.int32)[:, None, None]
    spike_selected = jnp.any(sequence_position == spike_position[None], axis=2).astype(jnp.float32)
    spike_log_decay = jnp.log(jax.random.uniform(random_subkeys[6], complete_shape, minval=0.55, maxval=0.8))
    return -baseline_decay_rate * block_scale_factor * random_noise + spike_selected * spike_log_decay


def shard_levels(rng, dims, cuts, smallest, top_value):
    def one(dim, parts):
        steps = jax.random.uniform(jax.random.fold_in(jax.random.fold_in(rng, 6), dim), (parts,), jnp.float32, smallest / len(cuts), top_value / len(cuts))
        return jnp.repeat(jnp.exp(steps), dims[dim] // parts).reshape((-1,) + (1,) * (len(dims) - dim - 1))

    gain = one(*cuts[0])
    for cut in cuts[1:]:
        gain = gain * one(*cut)
    return gain


def assign_block(rng, own, number, rows, count, top, most, slope):
    ranking = jax.random.permutation(rng, count)
    crowded, ordinary = shares(count, rows * top, most, slope, True), shares(count, rows * top, most, slope, False)
    places = jnp.arange(count)

    def named(tallies, rotation):
        used = int((tallies > 0).sum())
        fixed = max(1, used // 4)
        moved = fixed + (places - fixed + rotation * (used - fixed)) % max(1, count - fixed)
        return jnp.zeros((count,), jnp.int32).at[ranking[jnp.where(places < fixed, places, moved)]].set(jnp.asarray(tallies, jnp.int32))

    tallies = jnp.where(number % 4 == 0, named(crowded, number // 4), named(ordinary, number - number // 4 - 1))
    mixed = jax.random.permutation(jax.random.fold_in(own, 3), count)
    giver, sink = mixed[0:count // 2 * 2:2], mixed[1:count // 2 * 2:2]
    room = jnp.minimum(tallies[giver] - 1, most - tallies[sink]) // 2
    room = jnp.where((giver == ranking[0]) | (sink == ranking[0]) | (tallies[sink] == 0), 0, jnp.maximum(room, 0))
    moved = jax.random.randint(jax.random.fold_in(own, 4), (count // 2,), 0, 1 << 20) % (room + 1)
    tallies = tallies.at[giver].add(-moved).at[sink].add(moved)
    items = jnp.searchsorted(jnp.cumsum(tallies), jnp.arange(rows * top), side="right").astype(jnp.int32)
    table = items.reshape(top, rows).T
    table = table[jax.random.permutation(jax.random.fold_in(own, 1), rows)]
    rotation = jax.random.randint(jax.random.fold_in(own, 2), (rows, 1), 0, top)
    return jnp.take_along_axis(table, (jnp.arange(top)[None, :] + rotation) % top, axis=1)


def shares(number_of, total, reach, skew, full):
    loads = [(1 << 20) // math.isqrt(standing ** skew) + 1 for standing in range(1, number_of + 1)]
    largest = reach if full else min(reach, max(-(-total // number_of), total * loads[0] // sum(loads)))
    least = 1 if total - largest >= number_of - 1 else 0
    given, spare = [largest] + [least] * (number_of - 1), total - largest - least * (number_of - 1)
    while spare > 0:
        free = [i for i in range(1, number_of) if given[i] < largest] or [i for i in range(1, number_of) if given[i] < reach]
        whole, remaining = sum([loads[i] for i in free]), spare
        for i in free:
            extra = min(reach - given[i], max(1, remaining * loads[i] // whole), spare)
            given[i] = given[i] + extra
            spare = spare - extra
    return np.array(given)


def normal_values(rng, dims, spread, reach, cuts=(), held_as=jnp.bfloat16):
    values = jax.random.normal(rng, dims, jnp.float32) * spread
    if len(cuts) > 0:
        values = shard_levels(rng, dims, cuts, -0.22, 0.18) * values
    return jnp.clip(values, min=-reach, max=reach).astype(held_as)


def setup_inputs(seed: int = 0) -> dict:
    seeds = jax.random.split(jax.random.key(seed), 13)
    residual = normal_values(seeds[0], (SEQUENCE_LENGTH, D), 1.0, 6.0, ((0, 16), (1, 16)))
    ssm_values = normal_values(seeds[1], (SEQUENCE_LENGTH, D), 1.0, 6.0, ((0, 16), (1, 16)))
    ssm_keys = normal_values(seeds[2], (SEQUENCE_LENGTH, STATE), 1.0, 6.0, ((0, 16),))
    ssm_queries = normal_values(seeds[3], (SEQUENCE_LENGTH, STATE), (STATE * SEQUENCE_LENGTH) ** -0.5, 0.015625, ((0, 16),))
    log_decay = draw_log_decay(jax.random.fold_in(seeds[12], 71), 0)
    expert_ids_keys = jax.random.split(jax.random.fold_in(seeds[5], 1), SEQUENCE_LENGTH // TOK_DEV)
    expert_ids_turns = jax.random.permutation(jax.random.fold_in(seeds[5], 3), SEQUENCE_LENGTH // TOK_DEV)
    expert_ids = jax.vmap(lambda own, number: assign_block(jax.random.fold_in(seeds[5], 2), own, number, TOK_DEV, EXPERTS, 2, CAP, 2))(expert_ids_keys, expert_ids_turns).reshape((SEQUENCE_LENGTH, 2))
    gate_probs = jnp.clip(0.2 + 0.8 * jax.random.uniform(seeds[6], (SEQUENCE_LENGTH, 2), jnp.float32) ** shard_levels(seeds[6], (SEQUENCE_LENGTH, 2), ((0, 16),), -0.2, 0.2), 0.2, 1.0)
    norm_gain = jnp.clip(1.0 + 0.1 * jax.random.normal(seeds[7], (D,), jnp.float32), 0.5, 1.5)
    w_gate = normal_values(seeds[8], (EXPERTS, D, FW), D ** -0.5, 0.09375, ((0, 8), (2, 32)))
    w_up = normal_values(seeds[9], (EXPERTS, D, FW), D ** -0.5, 0.09375, ((0, 8), (2, 32)))
    w_down = normal_values(seeds[10], (EXPERTS, D, FW), FW ** -0.5, 0.0625, ((0, 8), (2, 32)))
    out_grad = normal_values(seeds[11], (SEQUENCE_LENGTH, D), 1.0, 6.0, ((0, 16), (1, 16)))
    return {"residual": residual, "ssm_values": ssm_values, "ssm_keys": ssm_keys, "ssm_queries": ssm_queries, "log_decay": log_decay, "expert_ids": expert_ids, "gate_probs": gate_probs, "norm_gain": norm_gain, "w_gate": w_gate, "w_up": w_up, "w_down": w_down, "out_grad": out_grad}


HIGH = lax.Precision.HIGHEST
EPS = 1e-05

def block_state(values, key_rows, log_decay):
    cumulative = jnp.cumsum(log_decay, axis=0)
    total_log = cumulative[-1]
    tail_decay = jnp.exp(total_log[None, :] - cumulative)
    weighted = tail_decay[:, :, None] * values
    state_local = jnp.einsum('shp,sn->hpn', weighted, key_rows, precision=HIGH)
    return (jnp.exp(total_log), state_local)

def block_output(values, key_rows, queries, log_decay, state_in):
    cumulative = jnp.cumsum(log_decay, axis=0)
    length = values.shape[0]
    row_index = lax.broadcasted_iota(jnp.int32, (length, length), 0)
    col_index = lax.broadcasted_iota(jnp.int32, (length, length), 1)
    causal = (row_index >= col_index)[None]
    cum_heads = cumulative.T
    log_gap = jnp.where(causal, cum_heads[:, :, None] - cum_heads[:, None, :], 0.0)
    decay_mat = jnp.where(causal, jnp.exp(log_gap), 0.0)
    scores = jnp.dot(queries, key_rows.T, precision=HIGH)
    inner_part = jnp.einsum('hts,shp->thp', decay_mat * scores[None], values, precision=HIGH)
    carried = jnp.einsum('tn,hpn->thp', queries, state_in, precision=HIGH)
    return inner_part + jnp.exp(cumulative)[:, :, None] * carried

def silu_parts(gate_act):
    sigmoid_val = jax.nn.sigmoid(gate_act)
    return (gate_act * sigmoid_val, sigmoid_val * (1.0 + gate_act * (1.0 - sigmoid_val)))

def route_slots(token_ids, expert_count):
    owners = token_ids.reshape(-1)
    onehot = (owners[:, None] == jnp.arange(expert_count, dtype=jnp.int32)[None, :]).astype(jnp.int32)
    rank_before = jnp.cumsum(onehot, axis=0) - onehot
    return (owners, lax.optimization_barrier(jnp.sum(rank_before * onehot, axis=1)).astype(jnp.int32))

def seq_output(values, key_rows, queries, log_decay):
    blocks = values.shape[0] // TOK_DEV

    def advance(state_in, pieces):
        block_vals, block_keys, block_queries, block_decay = pieces
        out_rows = block_output(block_vals, block_keys, block_queries, block_decay, state_in)
        decay_total, state_local = block_state(block_vals, block_keys, block_decay)
        return (decay_total[:, None, None] * state_in + state_local, out_rows)
    pieces = (values.reshape(blocks, TOK_DEV, HEADS, HDIM), key_rows.reshape(blocks, TOK_DEV, STATE), queries.reshape(blocks, TOK_DEV, STATE), log_decay.reshape(blocks, TOK_DEV, HEADS))
    start_state = jnp.zeros((HEADS, HDIM, STATE), jnp.float32)
    _, outputs = lax.scan(advance, start_state, pieces)
    return outputs.reshape(-1, HEADS, HDIM)

def grouped_sum(term_of_group, rows, width):
    groups = FW // FW_DEV

    def add_group(running, group):
        start = (group * FW_DEV).astype(jnp.int32)
        term = term_of_group(start)
        rounded = lax.optimization_barrier(term.astype(jnp.bfloat16))
        return (running + rounded.astype(jnp.float32), None)
    start_sum = jnp.zeros((rows, width), jnp.float32)
    total, _ = lax.scan(add_group, start_sum, jnp.arange(groups, dtype=jnp.int32))
    return total

def one_expert(pieces):
    got_rows, got_cot, gate_w, up_w, down_w = pieces
    rows = got_rows.shape[0]
    act_gate = jnp.dot(got_rows, gate_w, preferred_element_type=jnp.float32)
    act_up = jnp.dot(got_rows, up_w, preferred_element_type=jnp.float32)
    swish_val, swish_slope = silu_parts(act_gate)
    hidden_act = (swish_val * act_up).astype(jnp.bfloat16)

    def out_term(start):
        part_act = lax.dynamic_slice_in_dim(hidden_act, start, FW_DEV, 1)
        weight = lax.dynamic_slice_in_dim(down_w, start, FW_DEV, 1)
        return jnp.dot(part_act, weight.T, preferred_element_type=jnp.float32)
    expert_out = grouped_sum(out_term, rows, D).astype(jnp.bfloat16)
    grad_act = jnp.dot(got_cot, down_w, preferred_element_type=jnp.float32)
    grad_gate = (grad_act * act_up * swish_slope).astype(jnp.bfloat16)
    grad_up = (grad_act * swish_val).astype(jnp.bfloat16)

    def back_term(start):
        part_gate = lax.dynamic_slice_in_dim(grad_gate, start, FW_DEV, 1)
        part_up = lax.dynamic_slice_in_dim(grad_up, start, FW_DEV, 1)
        weight_gate = lax.dynamic_slice_in_dim(gate_w, start, FW_DEV, 1)
        weight_up = lax.dynamic_slice_in_dim(up_w, start, FW_DEV, 1)
        return jnp.dot(part_gate, weight_gate.T, preferred_element_type=jnp.float32) + jnp.dot(part_up, weight_up.T, preferred_element_type=jnp.float32)
    pair_back = grouped_sum(back_term, rows, D).astype(jnp.bfloat16)
    gate_grad = jnp.dot(got_rows.T, grad_gate, preferred_element_type=jnp.float32).astype(jnp.bfloat16)
    up_grad = jnp.dot(got_rows.T, grad_up, preferred_element_type=jnp.float32).astype(jnp.bfloat16)
    down_grad = jnp.dot(got_cot.T, hidden_act, preferred_element_type=jnp.float32).astype(jnp.bfloat16)
    return (expert_out, pair_back, gate_grad, up_grad, down_grad)

def reference(residual, ssm_values, ssm_keys, ssm_queries, log_decay, expert_ids, gate_probs, norm_gain, w_gate, w_up, w_down, out_grad):
    seq_values = ssm_values.astype(jnp.float32).reshape(SEQUENCE_LENGTH, HEADS, HDIM)
    seq_keys = ssm_keys.astype(jnp.float32)
    seq_queries = ssm_queries.astype(jnp.float32)
    mixer_out = seq_output(seq_values, seq_keys, seq_queries, log_decay)
    hidden = (residual.astype(jnp.float32) + mixer_out.reshape(SEQUENCE_LENGTH, D)).astype(jnp.bfloat16)
    hidden_f = hidden.astype(jnp.float32)
    inv_rms = lax.rsqrt(lax.optimization_barrier(jnp.mean(hidden_f * hidden_f, axis=1, keepdims=True)) + EPS)
    normed = (hidden_f * inv_rms * norm_gain).astype(jnp.bfloat16)
    block_ids = expert_ids.reshape(N_CTX, TOK_DEV, 2)
    owners, slot_index = jax.vmap(lambda ids_block: route_slots(ids_block, EXPERTS))(block_ids)
    ctx_number = lax.broadcasted_iota(jnp.int32, owners.shape, 0)
    flat_row = ctx_number * CAP + slot_index
    pair_rows = jnp.repeat(normed.reshape(N_CTX, TOK_DEV, D), 2, axis=1)
    dout_rows = jnp.repeat(out_grad.reshape(N_CTX, TOK_DEV, D), 2, axis=1)
    pair_prob = gate_probs.reshape(N_CTX, 2 * TOK_DEV)
    pair_cot = (pair_prob[..., None] * dout_rows.astype(jnp.float32)).astype(jnp.bfloat16)
    empty = jnp.zeros((EXPERTS, N_CTX * CAP, D), jnp.bfloat16)
    rows_buffer = empty.at[owners, flat_row].set(pair_rows)
    cot_buffer = empty.at[owners, flat_row].set(pair_cot)
    out_buffer, back_buffer, w_gate_grad, w_up_grad, w_down_grad = lax.map(one_expert, (rows_buffer, cot_buffer, w_gate, w_up, w_down))
    out_pairs = out_buffer[owners, flat_row]
    grad_probs = lax.optimization_barrier(jnp.sum(out_pairs.astype(jnp.float32) * dout_rows.astype(jnp.float32), axis=2)).reshape(SEQUENCE_LENGTH, 2)
    back_pairs = back_buffer[owners, flat_row].astype(jnp.float32)
    grad_normed = back_pairs.reshape(N_CTX, TOK_DEV, 2, D).sum(axis=2).reshape(SEQUENCE_LENGTH, D)
    scaled = grad_normed * norm_gain
    projection = lax.optimization_barrier(jnp.mean(hidden_f * scaled, axis=1, keepdims=True))
    grad_hidden = out_grad.astype(jnp.float32) + inv_rms * scaled - hidden_f * inv_rms ** 3 * projection
    grad_gain = lax.optimization_barrier(jnp.sum(grad_normed * hidden_f * inv_rms, axis=0))
    grad_residual = grad_hidden.astype(jnp.bfloat16)
    _, pull_back = jax.vjp(seq_output, seq_values, seq_keys, seq_queries, log_decay)
    values_grad, grad_keys, grad_queries, grad_decay = pull_back(grad_hidden.reshape(SEQUENCE_LENGTH, HEADS, HDIM))
    grad_values = values_grad.reshape(SEQUENCE_LENGTH, D).astype(jnp.bfloat16)
    return (grad_residual, grad_values, grad_keys, grad_queries, grad_decay, grad_probs, grad_gain, w_gate_grad, w_up_grad, w_down_grad)
```

```python
import jax
import jax.numpy as jnp
from jax import lax
from jax.experimental import pallas as pl
from jax.experimental.pallas import tpu as pltpu
from jax.sharding import PartitionSpec as P

HIGH = lax.Precision.HIGHEST
EPS = 1e-05
F32 = jnp.float32
BF16 = jnp.bfloat16


def dot(a, b, dims=((1,), (0,)), precision=None):
    return lax.dot_general(a, b, (dims, ((), ())), precision=precision, preferred_element_type=F32)


def head_map(heads, width):
    size = width // heads
    return (
        lax.broadcasted_iota(jnp.int32, (heads, width), 1) // size
        == lax.broadcasted_iota(jnp.int32, (heads, width), 0)
    ).astype(F32)


def lower_mask(n):
    return lax.broadcasted_iota(jnp.int32, (n, n), 0) >= lax.broadcasted_iota(jnp.int32, (n, n), 1)


def block_state(values, key_rows, log_decay):
    tri = lower_mask(values.shape[0]).astype(F32)
    spread = head_map(log_decay.shape[1], values.shape[1])
    cumulative = dot(tri, log_decay, precision=HIGH)
    total_log = cumulative[-1:]
    tail = dot(jnp.exp(total_log - cumulative), spread, precision=HIGH)
    return total_log, dot(key_rows, tail * values, ((0,), (0,)), HIGH)


def block_output(values, key_rows, queries, log_decay, state_in):
    length, width = values.shape
    heads = log_decay.shape[1]
    size = width // heads
    causal = lower_mask(length)
    tri = causal.astype(F32)
    cumulative = dot(tri, log_decay, precision=HIGH)
    cum_heads = dot(log_decay, tri, ((0,), (1,)), HIGH)
    scores = dot(queries, key_rows, ((1,), (1,)), HIGH)
    parts = []
    for h in range(heads):
        log_gap = jnp.where(causal, cumulative[:, h : h + 1] - cum_heads[h : h + 1, :], 0.0)
        decay_mat = jnp.where(causal, jnp.exp(log_gap), 0.0)
        parts.append(dot(decay_mat * scores, values[:, h * size : (h + 1) * size], precision=HIGH))
    carried = dot(queries, state_in, precision=HIGH)
    growth = dot(jnp.exp(cumulative), head_map(heads, width), precision=HIGH)
    return jnp.concatenate(parts, axis=1) + growth * carried


def split_rows(x, parts):
    rows = []
    for _ in range(parts):
        head = lax.reduce_precision(x, 8, 7)
        rows.append(head.astype(BF16))
        x = x - head
    return rows


def pad_rows(rows, count, width):
    block = jnp.concatenate(rows, axis=0)
    return jnp.pad(block, ((0, count - block.shape[0]), (0, width - block.shape[1])))


def swap(x, axis):
    return lax.all_to_all(x, axis, 0, 0, tiled=True)


def to_all(x, axis):
    return swap(jnp.broadcast_to(x[None], (lax.axis_size(axis),) + x.shape), axis)


def flat_rows(block):
    shape = block.shape
    return block.astype(F32).reshape(shape[0] * shape[1], shape[2])


def open_kernel(core, rows_ref, gain_ref, wg_ref, wu_ref, ag_ref, au_ref, ss_ref):
    rows = flat_rows(rows_ref[...])
    scaled = (rows * gain_ref[...]).astype(BF16)

    @pl.when(pl.program_id(0) == 0)
    def _():
        ag_ref[...] = jnp.zeros_like(ag_ref)
        au_ref[...] = jnp.zeros_like(au_ref)
        ss_ref[...] = jnp.zeros_like(ss_ref)

    ag_ref[...] += dot(scaled, wg_ref[...])
    au_ref[...] += dot(scaled, wu_ref[...])
    ss_ref[...] += jnp.broadcast_to(jnp.sum(rows * rows, axis=1, keepdims=True), ss_ref.shape)


def close_kernel(
    core, rows_ref, gain_ref, wg_ref, wu_ref, ag_in, au_in, ss_in, ga_ref,
    hact_ref, dg_ref, du_ref, dgi_ref, dui_ref, sc_ref, ag_ref, au_ref, ss_ref,
):
    rows = flat_rows(rows_ref[...])
    scaled = (rows * gain_ref[...]).astype(BF16)

    @pl.when(pl.program_id(0) == 0)
    def _():
        ag_ref[...] = ag_in[...]
        au_ref[...] = au_in[...]
        ss_ref[...] = ss_in[...]

    ag_ref[...] += dot(scaled, wg_ref[...])
    au_ref[...] += dot(scaled, wu_ref[...])
    ss_ref[...] += jnp.broadcast_to(jnp.sum(rows * rows, axis=1, keepdims=True), ss_ref.shape)

    @pl.when(pl.program_id(0) == pl.num_programs(0) - 1)
    def _():
        width = 2 * pl.num_programs(0) * rows.shape[1]
        inv = lax.rsqrt(ss_ref[:, :1] / width + EPS)
        act_gate = inv * ag_ref[...]
        act_up = inv * au_ref[...]
        grad_act = ga_ref[...]
        sig = jax.nn.sigmoid(act_gate)
        swish = act_gate * sig
        slope = sig * (1.0 + act_gate * (1.0 - sig))
        hact = (swish * act_up).astype(BF16)
        dg32 = grad_act * act_up * slope
        du32 = grad_act * swish
        dg = dg32.astype(BF16)
        du = du32.astype(BF16)
        hact_ref[...] = hact
        dg_ref[...] = dg
        du_ref[...] = du
        dgi_ref[...] = (inv * dg32).astype(BF16)
        dui_ref[...] = (inv * du32).astype(BF16)
        probs = jnp.sum(hact.astype(F32) * grad_act, axis=1, keepdims=True)
        inner = jnp.sum(
            dg.astype(F32) * act_gate + du.astype(F32) * act_up, axis=1, keepdims=True
        )
        lane = lax.broadcasted_iota(jnp.int32, sc_ref.shape, 1)
        sc_ref[...] = jnp.where(
            lane == 0, probs, jnp.where(lane == 1, inner, jnp.where(lane == 2, inv, 0.0))
        )


def cot_kernel(cot_ref, wd_ref, ga_ref):
    total = dot(flat_rows(cot_ref[:, 0]).astype(BF16), wd_ref[0])
    total += dot(flat_rows(cot_ref[:, 1]).astype(BF16), wd_ref[1])

    @pl.when(pl.program_id(0) == 0)
    def _():
        ga_ref[...] = total

    @pl.when(pl.program_id(0) > 0)
    def _():
        ga_ref[...] += total


def back_term(dg_ref, du_ref, wg_ref, wu_ref):
    return dot(dg_ref[...], wg_ref[...], ((1,), (1,))) + dot(
        du_ref[...], wu_ref[...], ((1,), (1,))
    )


def back_kernel(core, dg_ref, du_ref, wg_ref, wu_ref, out_ref):
    term = back_term(dg_ref, du_ref, wg_ref, wu_ref)
    out_ref[...] = term.reshape(out_ref.shape).astype(BF16)


def back_add_kernel(core, dg_ref, du_ref, wg_ref, wu_ref, other_ref, sc_ref, out_ref):
    slots = other_ref.shape[1]
    step = pl.program_id(0)
    term = back_term(dg_ref, du_ref, wg_ref, wu_ref).astype(BF16).astype(F32)
    both = term.reshape(other_ref.shape) + other_ref[...].astype(F32)
    out_ref[:, pl.ds(pl.multiple_of(step * slots, 8), slots), :] = both.astype(BF16)

    @pl.when(step == 0)
    def _():
        out_ref[:, pl.num_programs(0) * slots :, :] = sc_ref[...]


def grads_kernel(
    core, own_ref, oth_ref, cot_ref, gown_ref, goth_ref, dgi_ref, dui_ref, hact_ref,
    gate_ref, up_ref, down_ref,
):
    here = core[0]
    first = ((0,), (0,))
    for rows_ref, gain_ref, place in ((own_ref, gown_ref, here), (oth_ref, goth_ref, 1 - here)):
        scaled = (flat_rows(rows_ref[...]) * gain_ref[...]).astype(BF16)
        gate_ref[place] = dot(scaled, dgi_ref[...], first).astype(BF16)
        up_ref[place] = dot(scaled, dui_ref[...], first).astype(BF16)
    for place in range(2):
        cot = flat_rows(cot_ref[:, place]).astype(BF16)
        down_ref[place] = dot(cot, hact_ref[...], first).astype(BF16)


def whole(shape):
    return pl.BlockSpec(shape, lambda e, *_: (0,) * len(shape))


def per_device(
    residual,
    ssm_values,
    ssm_keys,
    ssm_queries,
    log_decay,
    expert_ids,
    gate_probs,
    norm_gain,
    w_gate,
    w_up,
    w_down,
    out_grad,
):
    tokens, feat = residual.shape
    heads = log_decay.shape[1]
    model_width, units = w_gate.shape[1:]
    ctx_count = lax.axis_size("ctx")
    exp_count = lax.axis_size("exp")
    capacity = 5 * tokens // (2 * exp_count)
    rows_all = ctx_count * capacity
    ctx_here = lax.axis_index("ctx")
    core = lax.axis_index("dp").astype(jnp.int32).reshape(1)
    other_core = [(0, 1), (1, 0)]

    values = ssm_values.astype(F32)
    key_rows = ssm_keys.astype(F32)
    queries = ssm_queries.astype(F32)
    (total_log, state_local), state_pull = jax.vjp(block_state, values, key_rows, log_decay)
    state_rows = state_local.shape[0]
    payload = jnp.concatenate(
        [state_local.astype(BF16), pad_rows(split_rows(total_log, 3), 8, feat)], axis=0
    )
    got = to_all(payload, "ctx")
    logs = jnp.sum(got[:, state_rows : state_rows + 3, :heads].astype(F32), axis=1)
    source = lax.broadcasted_iota(jnp.int32, (ctx_count, ctx_count), 0)
    between = lax.broadcasted_iota(jnp.int32, (ctx_count, ctx_count), 1)
    spread = head_map(heads, feat)
    rank = jnp.arange(ctx_count, dtype=jnp.int32)[:, None]
    before = ((between > source) & (between < ctx_here)).astype(F32)
    after = ((between < source) & (between > ctx_here)).astype(F32)
    gap_before = jnp.sum(before[:, :, None] * logs[None], axis=1)
    gap_after = jnp.sum(after[:, :, None] * logs[None], axis=1)
    weight_before = dot(
        jnp.where(rank < ctx_here, jnp.exp(gap_before), 0.0), spread, precision=HIGH
    )
    weight_after = dot(jnp.where(rank > ctx_here, jnp.exp(gap_after), 0.0), spread, precision=HIGH)
    state_in = jnp.sum(weight_before[:, None, :] * got[:, :state_rows].astype(F32), axis=0)

    ids = expert_ids.T
    probs = gate_probs.T
    experts = jnp.arange(exp_count, dtype=jnp.int32)[:, None]
    named = [ids[k][None, :] == experts for k in range(2)]
    member = named[0] | named[1]
    strict = (~lower_mask(tokens)).astype(BF16)
    order = dot(member.astype(BF16), strict).astype(jnp.int32)
    slot = lax.broadcasted_iota(jnp.int32, (exp_count, capacity, tokens), 1)
    chosen = (order[:, None, :] == slot) & member[:, None, :]
    select = chosen.astype(BF16).reshape(exp_count * capacity, tokens)
    prob_of = jnp.where(named[0], probs[0][None, :], jnp.where(named[1], probs[1][None, :], 0.0))
    prob_rows = jnp.sum(jnp.where(chosen, prob_of[:, None, :], 0.0), axis=2)

    cot = (dot(select, out_grad).reshape(exp_count, capacity, feat) * prob_rows[:, :, None]).astype(
        BF16
    )
    gain_rows = pad_rows(split_rows(norm_gain[None, :], 3), 8, feat)
    got_cot = swap(
        jnp.concatenate(
            [cot, jnp.broadcast_to(gain_rows[None], (exp_count,) + gain_rows.shape)], axis=1
        ),
        "exp",
    )
    gain_own = jnp.sum(got_cot[:, capacity : capacity + 3].astype(F32), axis=1)[:, None, :]
    gain_oth = lax.ppermute(gain_own, "dp", other_core)
    all_cot = lax.all_gather(
        got_cot[:, :capacity].reshape(exp_count * capacity, feat), ("ctx", "dp"), axis=0
    ).reshape(ctx_count, 2, exp_count, capacity, feat)

    mixer_out, output_pull = jax.vjp(
        block_output, values, key_rows, queries, log_decay, state_in
    )
    hidden = (residual.astype(F32) + mixer_out).astype(BF16)
    hidden_f = hidden.astype(F32)
    got_rows = swap(
        dot(select, hidden).astype(BF16).reshape(exp_count, capacity, feat), "exp"
    )
    own = to_all(got_rows, "ctx")
    oth = lax.ppermute(own, "dp", other_core)

    gate4 = w_gate.reshape(exp_count, 2, feat, units)
    up4 = w_up.reshape(exp_count, 2, feat, units)
    down4 = w_down.reshape(exp_count, 2, feat, units)
    rows_spec = pl.BlockSpec((ctx_count, None, capacity, feat), lambda e, *_: (0, e, 0, 0))
    cot_spec = pl.BlockSpec((ctx_count, 2, None, capacity, feat), lambda e, *_: (0, 0, e, 0, 0))
    gain_spec = pl.BlockSpec((None, 1, feat), lambda e, *_: (e, 0, 0))
    w_own = pl.BlockSpec((None, None, feat, units), lambda e, s: (e, s[0], 0, 0))
    w_oth = pl.BlockSpec((None, None, feat, units), lambda e, s: (e, 1 - s[0], 0, 0))
    w_pair = pl.BlockSpec((None, 2, feat, units), lambda e, *_: (e, 0, 0, 0))
    acts = whole((rows_all, units))
    sums = whole((rows_all, 128))
    acts_f = jax.ShapeDtypeStruct((rows_all, units), F32)
    acts_b = jax.ShapeDtypeStruct((rows_all, units), BF16)
    sums_f = jax.ShapeDtypeStruct((rows_all, 128), F32)

    def grid_of(n_scalars, in_specs, out_specs, scratch=()):
        return pltpu.PrefetchScalarGridSpec(
            num_scalar_prefetch=n_scalars,
            grid=(exp_count,),
            in_specs=in_specs,
            out_specs=out_specs,
            scratch_shapes=list(scratch),
        )

    grad_act = pl.pallas_call(
        cot_kernel, grid_spec=grid_of(0, [cot_spec, w_pair], acts), out_shape=acts_f, name="cot"
    )(all_cot, down4)
    ag, au, ss = pl.pallas_call(
        open_kernel,
        grid_spec=grid_of(1, [rows_spec, gain_spec, w_own, w_own], [acts, acts, sums]),
        out_shape=[acts_f, acts_f, sums_f],
        name="open",
    )(core, own, gain_own, gate4, up4)
    hact, dg, du, dgi, dui, scal = pl.pallas_call(
        close_kernel,
        grid_spec=grid_of(
            1,
            [rows_spec, gain_spec, w_oth, w_oth, acts, acts, sums, acts],
            [acts] * 5 + [sums],
            [
                pltpu.VMEM((rows_all, units), F32),
                pltpu.VMEM((rows_all, units), F32),
                pltpu.VMEM((rows_all, 128), F32),
            ],
        ),
        out_shape=[acts_b] * 5 + [sums_f],
        name="close",
    )(core, oth, gain_oth, gate4, up4, ag, au, ss, grad_act)
    small = scal[:, :8]
    small = small + lax.ppermute(small, "dp", other_core)
    small = small.reshape(ctx_count, capacity, 8).transpose(0, 2, 1)[:, :3]
    small = jnp.concatenate(
        [small[:, :2], small[:, 2:] * (0.5 / ctx_count)], axis=1
    )
    small_rows = jnp.pad(
        jnp.concatenate(split_rows(small, 2), axis=1), ((0, 0), (0, 2), (0, feat - capacity))
    )
    back_oth = pl.pallas_call(
        back_kernel,
        grid_spec=grid_of(1, [acts, acts, w_oth, w_oth], rows_spec),
        out_shape=jax.ShapeDtypeStruct((ctx_count, exp_count, capacity, feat), BF16),
        name="back_oth",
    )(core, dg, du, gate4, up4)
    back_got = lax.ppermute(back_oth, "dp", other_core)
    back_rows = exp_count * capacity
    back = pl.pallas_call(
        back_add_kernel,
        grid_spec=grid_of(
            1,
            [acts, acts, w_own, w_own, rows_spec, whole((ctx_count, 8, feat))],
            whole((ctx_count, back_rows + 8, feat)),
        ),
        out_shape=jax.ShapeDtypeStruct((ctx_count, back_rows + 8, feat), BF16),
        name="back_own",
    )(core, dg, du, gate4, up4, back_got, small_rows)
    gate_grad, up_grad, down_grad = pl.pallas_call(
        grads_kernel,
        grid_spec=grid_of(
            1,
            [rows_spec, rows_spec, cot_spec, gain_spec, gain_spec, acts, acts, acts],
            [w_pair] * 3,
        ),
        out_shape=[jax.ShapeDtypeStruct(gate4.shape, BF16)] * 3,
        name="grads",
    )(core, own, oth, all_cot, gain_own, gain_oth, dgi, dui, hact)

    summed = jnp.sum(swap(back, "ctx").astype(F32), axis=0)
    small = summed[back_rows : back_rows + 3] + summed[back_rows + 3 : back_rows + 6]
    small_rows = pad_rows(split_rows(small, 2), 8, feat)
    got_back = swap(
        jnp.concatenate(
            [
                summed[:back_rows].astype(BF16).reshape(exp_count, capacity, feat),
                jnp.broadcast_to(small_rows[None], (exp_count,) + small_rows.shape),
            ],
            axis=1,
        ),
        "exp",
    )
    grad_normed = dot(select, got_back[:, :capacity].reshape(back_rows, feat), ((0,), (0,)))
    small = got_back[:, capacity:, :capacity].astype(F32)
    small = small[:, :3] + small[:, 3:6]
    per_expert = lax.dot_general(
        small,
        chosen.astype(F32),
        (((2,), (1,)), ((0,), (0,))),
        precision=HIGH,
        preferred_element_type=F32,
    )
    grad_probs = jnp.stack(
        [
            jnp.sum(jnp.where(named[k], per_expert[:, 0], 0.0), axis=0) / probs[k]
            for k in range(2)
        ],
        axis=1,
    )
    inner = jnp.sum(per_expert[:, 1], axis=0)[:, None]
    inv_rms = (jnp.sum(per_expert[:, 2], axis=0) * 0.5)[:, None]
    scaled = grad_normed * norm_gain[None, :]
    grad_hidden = (
        out_grad.astype(F32)
        + inv_rms * scaled
        - hidden_f * (inv_rms * inv_rms * inner / model_width)
    )
    gain_part = jnp.sum(grad_normed * hidden_f * inv_rms, axis=0, keepdims=True)

    vals_first, keys_first, queries_part, decay_first, carry_cot = output_pull(grad_hidden)
    got_carry = to_all(
        jnp.concatenate(
            [carry_cot.astype(BF16), pad_rows(split_rows(gain_part, 3), 8, feat)], axis=0
        ),
        "ctx",
    )
    grad_state = jnp.sum(weight_after[:, None, :] * got_carry[:, :state_rows].astype(F32), axis=0)
    grad_gain = jnp.sum(got_carry[:, state_rows : state_rows + 3].astype(F32), axis=(0, 1))
    grad_total = dot(
        jnp.sum(grad_state * state_in, axis=0, keepdims=True), spread, ((1,), (1,)), HIGH
    ) * jnp.exp(total_log)
    vals_second, keys_second, decay_second = state_pull((grad_total, grad_state))
    both = jnp.concatenate([keys_first + keys_second, queries_part], axis=1).astype(BF16)
    both = (both.astype(F32) + lax.ppermute(both, "dp", other_core).astype(F32)).astype(BF16)
    both = jnp.sum(to_all(both, "exp").astype(F32), axis=0)
    return (
        grad_hidden.astype(BF16),
        (vals_first + vals_second).astype(BF16),
        both[:, :state_rows],
        both[:, state_rows:],
        decay_first + decay_second,
        grad_probs,
        grad_gain,
        gate_grad.reshape(w_gate.shape),
        up_grad.reshape(w_up.shape),
        down_grad.reshape(w_down.shape),
    )


def solution(mesh):
    rows = P("ctx", ("exp", "dp"))
    weights = P("exp", None, ("ctx", "dp"))
    ctx = P("ctx", None)
    gain = P(("exp", "dp"))
    return jax.shard_map(
        per_device,
        mesh=mesh,
        in_specs=(
            rows, rows, ctx, ctx, rows, ctx, ctx, gain, weights, weights, weights, rows,
        ),
        out_specs=(rows, rows, ctx, ctx, rows, ctx, gain, weights, weights, weights),
        check_vma=False,
    )
```

```python
import functools

import jax
import jax.numpy as jnp
from jax import lax
from jax.experimental import pallas as pl
from jax.experimental.pallas import tpu as pltpu
from jax.sharding import PartitionSpec as P


HIGH = lax.Precision.HIGHEST
EPS = 1e-05
F32 = jnp.float32
BF16 = jnp.bfloat16


def dot(a, b, dims=((1,), (0,)), precision=None):
    return lax.dot_general(a, b, (dims, ((), ())), precision=precision, preferred_element_type=F32)


def head_map(heads, width):
    size = width // heads
    return (
        lax.broadcasted_iota(jnp.int32, (heads, width), 1) // size
        == lax.broadcasted_iota(jnp.int32, (heads, width), 0)
    ).astype(F32)


def lower_mask(n):
    return lax.broadcasted_iota(jnp.int32, (n, n), 0) >= lax.broadcasted_iota(jnp.int32, (n, n), 1)


def block_state(values, key_rows, log_decay):
    tri = lower_mask(values.shape[0]).astype(F32)
    spread = head_map(log_decay.shape[1], values.shape[1])
    cumulative = dot(tri, log_decay, precision=HIGH)
    total_log = cumulative[-1:]
    tail = dot(jnp.exp(total_log - cumulative), spread, precision=HIGH)
    return total_log, dot(key_rows, tail * values, ((0,), (0,)), HIGH)


def block_output(values, key_rows, queries, log_decay, state_in):
    length, width = values.shape
    heads = log_decay.shape[1]
    size = width // heads
    causal = lower_mask(length)
    tri = causal.astype(F32)
    cumulative = dot(tri, log_decay, precision=HIGH)
    cum_heads = dot(log_decay, tri, ((0,), (1,)), HIGH)
    scores = dot(queries, key_rows, ((1,), (1,)), HIGH)
    parts = []
    for h in range(heads):
        log_gap = jnp.where(causal, cumulative[:, h : h + 1] - cum_heads[h : h + 1, :], 0.0)
        decay_mat = jnp.where(causal, jnp.exp(log_gap), 0.0)
        parts.append(dot(decay_mat * scores, values[:, h * size : (h + 1) * size], precision=HIGH))
    carried = dot(queries, state_in, precision=HIGH)
    growth = dot(jnp.exp(cumulative), head_map(heads, width), precision=HIGH)
    return jnp.concatenate(parts, axis=1) + growth * carried


def split_rows(x, parts):
    rows = []
    for _ in range(parts):
        head = lax.reduce_precision(x, 8, 7)
        rows.append(head.astype(BF16))
        x = x - head
    return rows


def pad_rows(rows, count, width):
    block = jnp.concatenate(rows, axis=0)
    return jnp.pad(block, ((0, count - block.shape[0]), (0, width - block.shape[1])))


def swap(x, axis):
    return lax.all_to_all(x, axis, 0, 0, tiled=True)


def to_all(x, axis):
    return swap(jnp.broadcast_to(x[None], (lax.axis_size(axis),) + x.shape), axis)


def stacked(ref):
    return ref[...].reshape(ref.shape[0] * ref.shape[1], ref.shape[2])


def square_sums(rows_ref, like):
    total = None
    for start in range(0, rows_ref.shape[1], like.shape[1]):
        part = rows_ref[:, start : start + like.shape[1]].astype(F32)
        total = part * part if total is None else total + part * part
    return jnp.broadcast_to(jnp.sum(total, axis=1, keepdims=True), like.shape)


def open_kernel(core, rows_ref, wg_ref, wu_ref, ag_ref, au_ref, ss_ref):
    ag_ref[...] = dot(rows_ref[...], stacked(wg_ref))
    au_ref[...] = dot(rows_ref[...], stacked(wu_ref))
    ss_ref[...] = square_sums(rows_ref, ss_ref)


def close_kernel(
    core, rows_ref, wg_ref, wu_ref, ag_in, au_in, ss_in, ga_ref,
    hact_ref, dg_ref, du_ref, dgi_ref, dui_ref, sc_ref,
):
    width = 2 * rows_ref.shape[1]
    total = (ss_in[...] + square_sums(rows_ref, ss_in))[:, :1]
    inv = lax.rsqrt(total / width + EPS)
    act_gate = inv * (ag_in[...] + dot(rows_ref[...], stacked(wg_ref)))
    act_up = inv * (au_in[...] + dot(rows_ref[...], stacked(wu_ref)))
    grad_act = ga_ref[...]
    sig = jax.nn.sigmoid(act_gate)
    swish = act_gate * sig
    slope = sig * (1.0 + act_gate * (1.0 - sig))
    hact = (swish * act_up).astype(BF16)
    dg32 = grad_act * act_up * slope
    du32 = grad_act * swish
    dg = dg32.astype(BF16)
    du = du32.astype(BF16)
    hact_ref[...] = hact
    dg_ref[...] = dg
    du_ref[...] = du
    dgi_ref[...] = (inv * dg32).astype(BF16)
    dui_ref[...] = (inv * du32).astype(BF16)
    probs = jnp.sum(hact.astype(F32) * grad_act, axis=1, keepdims=True)
    inner = jnp.sum(dg.astype(F32) * act_gate + du.astype(F32) * act_up, axis=1, keepdims=True)
    lane = lax.broadcasted_iota(jnp.int32, sc_ref.shape, 1)
    sc_ref[...] = jnp.where(
        lane == 0, probs, jnp.where(lane == 1, inner, jnp.where(lane == 2, inv, 0.0))
    )


def cot_kernel(core, own_ref, oth_ref, w_own_ref, w_oth_ref, ga_ref):
    ga_ref[...] = dot(own_ref[...], stacked(w_own_ref)) + dot(oth_ref[...], stacked(w_oth_ref))


def back_term(dg_ref, du_ref, wg_ref, wu_ref, block):
    return dot(dg_ref[...], wg_ref[block], ((1,), (1,))) + dot(
        du_ref[...], wu_ref[block], ((1,), (1,))
    )


def back_kernel(core, dg_ref, du_ref, wg_ref, wu_ref, out_ref):
    feat = wg_ref.shape[1]
    for block in range(wg_ref.shape[0]):
        term = back_term(dg_ref, du_ref, wg_ref, wu_ref, block)
        out_ref[:, block * feat : (block + 1) * feat] = term.astype(BF16)


def back_add_kernel(
    ctx_count, core, dg_ref, du_ref, wg_ref, wu_ref, other_ref, sc_ref, sc_other_ref, out_ref
):
    feat = wg_ref.shape[1]
    width = wg_ref.shape[0] * feat
    for block in range(wg_ref.shape[0]):
        lanes = slice(block * feat, (block + 1) * feat)
        term = back_term(dg_ref, du_ref, wg_ref, wu_ref, block).astype(BF16).astype(F32)
        out_ref[:, lanes] = (term + other_ref[:, lanes].astype(F32)).astype(BF16)
    small = sc_ref[...] + sc_other_ref[...]
    lane = lax.broadcasted_iota(jnp.int32, small.shape, 1)
    small = jnp.where(lane == 2, small * (0.5 / ctx_count), small)
    head = small.astype(BF16).astype(F32)
    tail = pltpu.roll(small - head, 3, 1)
    out_ref[:, width:] = jnp.where(lane < 3, head, jnp.where(lane < 6, tail, 0.0)).astype(BF16)


def grads_kernel(
    core, own_ref, oth_ref, cot_own_ref, cot_oth_ref, gown_ref, goth_ref, dgi_ref, dui_ref,
    hact_ref, gate_ref, up_ref, down_ref,
):
    here = core[0]
    first = ((0,), (0,))
    for rows_ref, cot_ref, gain_ref, place in (
        (own_ref, cot_own_ref, gown_ref, here),
        (oth_ref, cot_oth_ref, goth_ref, 1 - here),
    ):
        scaled = (rows_ref[...].astype(F32) * gain_ref[...]).astype(BF16)
        gate_ref[place] = dot(scaled, dgi_ref[...], first).astype(BF16)
        up_ref[place] = dot(scaled, dui_ref[...], first).astype(BF16)
        down_ref[place] = dot(cot_ref[...], hact_ref[...], first).astype(BF16)


def sums_kernel(got_ref, out_ref):
    feat = out_ref.shape[2] - 128
    count = out_ref.shape[0]

    def total(start, width):
        acc = got_ref[0, :, start : start + width].astype(F32)
        for block in range(1, got_ref.shape[0]):
            acc += got_ref[block, :, start : start + width].astype(F32)
        return acc

    small = total(count * feat, 128)
    lane = lax.broadcasted_iota(jnp.int32, small.shape, 1)
    small = jnp.where(lane < 3, small + pltpu.roll(small, 125, 1), 0.0)
    head = small.astype(BF16).astype(F32)
    small = (head + pltpu.roll(small - head, 3, 1)).astype(BF16)
    for block in range(count):
        out_ref[block, :, :feat] = total(block * feat, feat).astype(BF16)
        out_ref[block, :, feat:] = small


def whole(shape):
    return pl.BlockSpec(shape, lambda e, *_: (0,) * len(shape))


def side_by_side(blocks):
    return jnp.concatenate([blocks[e] for e in range(blocks.shape[0])], axis=1)


def per_device(
    residual,
    ssm_values,
    ssm_keys,
    ssm_queries,
    log_decay,
    expert_ids,
    gate_probs,
    norm_gain,
    w_gate,
    w_up,
    w_down,
    out_grad,
):
    tokens, feat = residual.shape
    heads = log_decay.shape[1]
    model_width, units = w_gate.shape[1:]
    ctx_count = lax.axis_size("ctx")
    exp_count = lax.axis_size("exp")
    capacity = 5 * tokens // (2 * exp_count)
    rows_all = ctx_count * capacity
    ctx_here = lax.axis_index("ctx")
    core = lax.axis_index("dp").astype(jnp.int32).reshape(1)
    other_core = [(0, 1), (1, 0)]

    values = ssm_values.astype(F32)
    key_rows = ssm_keys.astype(F32)
    queries = ssm_queries.astype(F32)
    (total_log, state_local), state_pull = jax.vjp(block_state, values, key_rows, log_decay)
    state_rows = state_local.shape[0]
    payload = jnp.concatenate(
        [state_local.astype(BF16), pad_rows(split_rows(total_log, 3), 8, feat)], axis=0
    )
    got = to_all(payload, "ctx")
    logs = jnp.sum(got[:, state_rows : state_rows + 3, :heads].astype(F32), axis=1)
    source = lax.broadcasted_iota(jnp.int32, (ctx_count, ctx_count), 0)
    between = lax.broadcasted_iota(jnp.int32, (ctx_count, ctx_count), 1)
    spread = head_map(heads, feat)
    rank = jnp.arange(ctx_count, dtype=jnp.int32)[:, None]
    before = ((between > source) & (between < ctx_here)).astype(F32)
    after = ((between < source) & (between > ctx_here)).astype(F32)
    gap_before = jnp.sum(before[:, :, None] * logs[None], axis=1)
    gap_after = jnp.sum(after[:, :, None] * logs[None], axis=1)
    weight_before = dot(
        jnp.where(rank < ctx_here, jnp.exp(gap_before), 0.0), spread, precision=HIGH
    )
    weight_after = dot(jnp.where(rank > ctx_here, jnp.exp(gap_after), 0.0), spread, precision=HIGH)
    state_in = jnp.sum(weight_before[:, None, :] * got[:, :state_rows].astype(F32), axis=0)

    ids = expert_ids.T
    probs = gate_probs.T
    experts = jnp.arange(exp_count, dtype=jnp.int32)[:, None]
    named = [ids[k][None, :] == experts for k in range(2)]
    member = named[0] | named[1]
    strict = (~lower_mask(tokens)).astype(BF16)
    order = dot(member.astype(BF16), strict).astype(jnp.int32)
    slot = lax.broadcasted_iota(jnp.int32, (exp_count, capacity, tokens), 1)
    chosen = (order[:, None, :] == slot) & member[:, None, :]
    select = chosen.astype(BF16).reshape(exp_count * capacity, tokens)
    select_each = jnp.concatenate(
        [
            (chosen & named[k][:, None, :]).astype(BF16).reshape(exp_count * capacity, tokens)
            for k in range(2)
        ],
        axis=1,
    )
    prob_of = jnp.where(named[0], probs[0][None, :], jnp.where(named[1], probs[1][None, :], 0.0))
    prob_rows = jnp.sum(jnp.where(chosen, prob_of[:, None, :], 0.0), axis=2)

    cot = (dot(select, out_grad).reshape(exp_count, capacity, feat) * prob_rows[:, :, None]).astype(
        BF16
    )
    gain_rows = pad_rows(split_rows(norm_gain[None, :], 3), 8, feat)
    cot_payload = jnp.concatenate(
        [cot, jnp.broadcast_to(gain_rows[None], (exp_count,) + gain_rows.shape)], axis=1
    )
    got_cot = swap(cot_payload, "exp")
    gain_own = jnp.sum(got_cot[:, capacity : capacity + 3].astype(F32), axis=1)
    gain_oth = lax.ppermute(gain_own, "dp", other_core)
    gain4 = jnp.where(
        core[0] == 0,
        jnp.stack([gain_own, gain_oth], axis=1),
        jnp.stack([gain_oth, gain_own], axis=1),
    )
    gate4 = w_gate.reshape(exp_count, 2, feat, units)
    up4 = w_up.reshape(exp_count, 2, feat, units)
    down4 = w_down.reshape(exp_count, 2, feat, units)
    gate_scaled = (gate4.astype(F32) * gain4[:, :, :, None]).astype(BF16)
    up_scaled = (up4.astype(F32) * gain4[:, :, :, None]).astype(BF16)
    wide = exp_count * feat
    rows_all = ctx_count * capacity
    cot_own = lax.all_gather(side_by_side(got_cot[:, :capacity]), "ctx", axis=0).reshape(
        rows_all, wide
    )
    cot_oth = lax.ppermute(cot_own, "dp", other_core)

    mixer_out, output_pull = jax.vjp(
        block_output, values, key_rows, queries, log_decay, state_in
    )
    hidden = (residual.astype(F32) + mixer_out).astype(BF16)
    hidden_f = hidden.astype(F32)
    got_rows = swap(
        dot(select, hidden).astype(BF16).reshape(exp_count, capacity, feat), "exp"
    )
    own = to_all(side_by_side(got_rows), "ctx").reshape(rows_all, wide)
    oth = lax.ppermute(own, "dp", other_core)

    split = 2
    part = rows_all // split
    rows_spec = pl.BlockSpec((part, wide), lambda i, *_: (i, 0))
    acts = pl.BlockSpec((part, units), lambda i, *_: (i, 0))
    sums = pl.BlockSpec((part, 128), lambda i, *_: (i, 0))
    w_own = pl.BlockSpec((exp_count, None, feat, units), lambda i, s: (0, s[0], 0, 0))
    w_oth = pl.BlockSpec((exp_count, None, feat, units), lambda i, s: (0, 1 - s[0], 0, 0))
    acts_f = jax.ShapeDtypeStruct((rows_all, units), F32)
    acts_b = jax.ShapeDtypeStruct((rows_all, units), BF16)
    sums_f = jax.ShapeDtypeStruct((rows_all, 128), F32)

    def grid_of(n_scalars, steps, in_specs, out_specs):
        return pltpu.PrefetchScalarGridSpec(
            num_scalar_prefetch=n_scalars,
            grid=(steps,),
            in_specs=in_specs,
            out_specs=out_specs,
        )

    grad_act = pl.pallas_call(
        cot_kernel,
        grid_spec=grid_of(1, split, [rows_spec, rows_spec, w_own, w_oth], acts),
        out_shape=acts_f,
        name="cot",
    )(core, cot_own, cot_oth, down4, down4)
    ag, au, ss = pl.pallas_call(
        open_kernel,
        grid_spec=grid_of(1, split, [rows_spec, w_own, w_own], [acts, acts, sums]),
        out_shape=[acts_f, acts_f, sums_f],
        name="open",
    )(core, own, gate_scaled, up_scaled)
    hact, dg, du, dgi, dui, scal = pl.pallas_call(
        close_kernel,
        grid_spec=grid_of(
            1,
            split,
            [rows_spec, w_oth, w_oth, acts, acts, sums, acts],
            [acts] * 5 + [sums],
        ),
        out_shape=[acts_b] * 5 + [sums_f],
        name="close",
    )(core, oth, gate_scaled, up_scaled, ag, au, ss, grad_act)
    scal_got = lax.ppermute(scal, "dp", other_core)
    back_oth = pl.pallas_call(
        back_kernel,
        grid_spec=grid_of(1, split, [acts, acts, w_oth, w_oth], rows_spec),
        out_shape=jax.ShapeDtypeStruct((rows_all, wide), BF16),
        name="back_oth",
    )(core, dg, du, gate4, up4)
    back_got = lax.ppermute(back_oth, "dp", other_core)
    back = pl.pallas_call(
        functools.partial(back_add_kernel, ctx_count),
        grid_spec=grid_of(
            1,
            split,
            [acts, acts, w_own, w_own, rows_spec, sums, sums],
            pl.BlockSpec((part, wide + 128), lambda i, *_: (i, 0)),
        ),
        out_shape=jax.ShapeDtypeStruct((rows_all, wide + 128), BF16),
        name="back_own",
    )(core, dg, du, gate4, up4, back_got, scal, scal_got)
    columns = pl.BlockSpec((rows_all, feat), lambda e, *_: (0, e))
    gain_spec = pl.BlockSpec((None, 1, feat), lambda e, *_: (e, 0, 0))
    w_pair = pl.BlockSpec((None, 2, feat, units), lambda e, *_: (e, 0, 0, 0))
    acts_all = whole((rows_all, units))
    gate_grad, up_grad, down_grad = pl.pallas_call(
        grads_kernel,
        grid_spec=grid_of(
            1,
            exp_count,
            [
                columns,
                columns,
                columns,
                columns,
                gain_spec,
                gain_spec,
                acts_all,
                acts_all,
                acts_all,
            ],
            [w_pair] * 3,
        ),
        out_shape=[jax.ShapeDtypeStruct(gate4.shape, BF16)] * 3,
        name="grads",
    )(
        core, own, oth, cot_own, cot_oth, gain_own[:, None], gain_oth[:, None], dgi, dui, hact
    )

    got_sums = swap(back.reshape(ctx_count, capacity, wide + 128), "ctx")
    summed = pl.pallas_call(
        sums_kernel,
        out_shape=jax.ShapeDtypeStruct((exp_count, capacity, feat + 128), BF16),
        name="sums",
    )(got_sums)
    got_back = swap(summed, "exp").reshape(exp_count * capacity, feat + 128)
    grad_normed = dot(select, got_back[:, :feat], ((0,), (0,)))
    small = dot(select_each, got_back[:, feat:], ((0,), (0,)))
    small = small[:, :3] + small[:, 3:6]
    grad_probs = (
        jnp.concatenate([small[:tokens, :1], small[tokens:, :1]], axis=1) / gate_probs
    )
    inner = small[:tokens, 1:2] + small[tokens:, 1:2]
    inv_rms = small[:tokens, 2:3]
    scaled = grad_normed * norm_gain[None, :]
    grad_hidden = (
        out_grad.astype(F32)
        + inv_rms * scaled
        - hidden_f * (inv_rms * inv_rms * inner / model_width)
    )
    gain_part = jnp.sum(grad_normed * hidden_f * inv_rms, axis=0, keepdims=True)

    vals_first, keys_first, queries_part, decay_first, carry_cot = output_pull(grad_hidden)
    got_carry = to_all(
        jnp.concatenate(
            [carry_cot.astype(BF16), pad_rows(split_rows(gain_part, 3), 8, feat)], axis=0
        ),
        "ctx",
    )
    grad_state = jnp.sum(weight_after[:, None, :] * got_carry[:, :state_rows].astype(F32), axis=0)
    grad_gain = jnp.sum(got_carry[:, state_rows : state_rows + 3].astype(F32), axis=(0, 1))
    grad_total = dot(
        jnp.sum(grad_state * state_in, axis=0, keepdims=True), spread, ((1,), (1,)), HIGH
    ) * jnp.exp(total_log)
    vals_second, keys_second, decay_second = state_pull((grad_total, grad_state))
    both = jnp.concatenate([keys_first + keys_second, queries_part], axis=1).astype(BF16)
    both = (both.astype(F32) + lax.ppermute(both, "dp", other_core).astype(F32)).astype(BF16)
    both = jnp.sum(to_all(both, "exp").astype(F32), axis=0)
    return (
        grad_hidden.astype(BF16),
        (vals_first + vals_second).astype(BF16),
        both[:, :state_rows],
        both[:, state_rows:],
        decay_first + decay_second,
        grad_probs,
        grad_gain,
        gate_grad.reshape(w_gate.shape),
        up_grad.reshape(w_up.shape),
        down_grad.reshape(w_down.shape),
    )


def solution(mesh):
    rows = P("ctx", ("exp", "dp"))
    weights = P("exp", None, ("ctx", "dp"))
    ctx = P("ctx", None)
    gain = P(("exp", "dp"))
    return jax.shard_map(
        per_device,
        mesh=mesh,
        in_specs=(
            rows, rows, ctx, ctx, rows, ctx, ctx, gain, weights, weights, weights, rows,
        ),
        out_specs=(rows, rows, ctx, ctx, rows, ctx, gain, weights, weights, weights),
        check_vma=False,
    )
```

```python
import functools

import jax
import jax.numpy as jnp
from jax import lax
from jax.experimental import pallas as pl
from jax.experimental.pallas import tpu as pltpu
from jax.sharding import PartitionSpec as P


HIGH = lax.Precision.HIGHEST
EPS = 1e-05
F32 = jnp.float32
BF16 = jnp.bfloat16


def dot(a, b, dims=((1,), (0,)), precision=None):
    return lax.dot_general(a, b, (dims, ((), ())), precision=precision, preferred_element_type=F32)


def head_map(heads, width):
    size = width // heads
    return (
        lax.broadcasted_iota(jnp.int32, (heads, width), 1) // size
        == lax.broadcasted_iota(jnp.int32, (heads, width), 0)
    ).astype(F32)


def lower_mask(n):
    return lax.broadcasted_iota(jnp.int32, (n, n), 0) >= lax.broadcasted_iota(jnp.int32, (n, n), 1)


def block_state(values, key_rows, log_decay):
    tri = lower_mask(values.shape[0]).astype(F32)
    spread = head_map(log_decay.shape[1], values.shape[1])
    cumulative = dot(tri, log_decay, precision=HIGH)
    total_log = cumulative[-1:]
    tail = dot(jnp.exp(total_log - cumulative), spread, precision=HIGH)
    return total_log, dot(key_rows, tail * values, ((0,), (0,)), HIGH)


def block_output(values, key_rows, queries, log_decay, state_in):
    length, width = values.shape
    heads = log_decay.shape[1]
    size = width // heads
    causal = lower_mask(length)
    tri = causal.astype(F32)
    cumulative = dot(tri, log_decay, precision=HIGH)
    cum_heads = dot(log_decay, tri, ((0,), (1,)), HIGH)
    scores = dot(queries, key_rows, ((1,), (1,)), HIGH)
    parts = []
    for h in range(heads):
        log_gap = jnp.where(causal, cumulative[:, h : h + 1] - cum_heads[h : h + 1, :], 0.0)
        decay_mat = jnp.where(causal, jnp.exp(log_gap), 0.0)
        parts.append(dot(decay_mat * scores, values[:, h * size : (h + 1) * size], precision=HIGH))
    carried = dot(queries, state_in, precision=HIGH)
    growth = dot(jnp.exp(cumulative), head_map(heads, width), precision=HIGH)
    return jnp.concatenate(parts, axis=1) + growth * carried


def split_rows(x, parts):
    rows = []
    for _ in range(parts):
        head = lax.reduce_precision(x, 8, 7)
        rows.append(head.astype(BF16))
        x = x - head
    return rows


def pad_rows(rows, count, width):
    block = jnp.concatenate(rows, axis=0)
    return jnp.pad(block, ((0, count - block.shape[0]), (0, width - block.shape[1])))


def swap(x, axis):
    return lax.all_to_all(x, axis, 0, 0, tiled=True)


def to_all(x, axis):
    return swap(jnp.broadcast_to(x[None], (lax.axis_size(axis),) + x.shape), axis)


SIDE = 4


def along_y(step):
    return [
        (y * SIDE + x, (y + step) % SIDE * SIDE + x) for y in range(SIDE) for x in range(SIDE)
    ]


def along_x(step):
    return [
        (y * SIDE + x, y * SIDE + (x + step) % SIDE) for y in range(SIDE) for x in range(SIDE)
    ]


def gather_rows(block):
    def spread(x, groups):
        return lax.all_to_all(
            jnp.broadcast_to(x[None], (SIDE,) + x.shape),
            "ctx",
            0,
            0,
            tiled=True,
            axis_index_groups=groups,
        )

    row = spread(block, [[y * SIDE + x for x in range(SIDE)] for y in range(SIDE)])
    return spread(row, [[y * SIDE + x for y in range(SIDE)] for x in range(SIDE)])


def gather_cot(block):
    here = lax.axis_index("ctx")
    y, x = here // SIDE, here % SIDE
    put = lax.dynamic_update_slice
    above = [lax.ppermute(block, "ctx", along_y(step)) for step in (1, 2, 3)]
    column = jnp.broadcast_to(block[None], (SIDE,) + block.shape)
    for step, piece in zip((1, 2, 3), above):
        column = put(column, piece[None], ((y + SIDE - step) % SIDE, 0, 0))
    left = lax.ppermute(column, "ctx", along_x(1))
    right = lax.ppermute(column, "ctx", along_x(3))
    half = SIDE // 2
    far_low = lax.ppermute(left[:half], "ctx", along_x(1))
    far_high = lax.ppermute(right[half:], "ctx", along_x(3))
    full = jnp.broadcast_to(column[:, None], (SIDE,) + column.shape)
    full = put(full, left[:, None], (0, (x + 3) % SIDE, 0, 0))
    full = put(full, right[:, None], (0, (x + 1) % SIDE, 0, 0))
    full = put(full, far_low[:, None], (0, (x + 2) % SIDE, 0, 0))
    return put(full, far_high[:, None], (half, (x + 2) % SIDE, 0, 0))


def stacked(ref):
    return ref[...].reshape(ref.shape[0] * ref.shape[1], ref.shape[2])


def square_sums(rows_ref, like):
    total = None
    for start in range(0, rows_ref.shape[1], like.shape[1]):
        part = rows_ref[:, start : start + like.shape[1]].astype(F32)
        total = part * part if total is None else total + part * part
    return jnp.broadcast_to(jnp.sum(total, axis=1, keepdims=True), like.shape)


def open_kernel(core, rows_ref, wg_ref, wu_ref, ag_ref, au_ref, ss_ref):
    ag_ref[...] = dot(rows_ref[...], stacked(wg_ref))
    au_ref[...] = dot(rows_ref[...], stacked(wu_ref))
    ss_ref[...] = square_sums(rows_ref, ss_ref)


def close_kernel(
    core, rows_ref, wg_ref, wu_ref, ag_in, au_in, ss_in, ga_ref,
    hact_ref, dg_ref, du_ref, dgi_ref, dui_ref, sc_ref,
):
    width = 2 * rows_ref.shape[1]
    total = (ss_in[...] + square_sums(rows_ref, ss_in))[:, :1]
    inv = lax.rsqrt(total / width + EPS)
    act_gate = inv * (ag_in[...] + dot(rows_ref[...], stacked(wg_ref)))
    act_up = inv * (au_in[...] + dot(rows_ref[...], stacked(wu_ref)))
    grad_act = ga_ref[...]
    sig = jax.nn.sigmoid(act_gate)
    swish = act_gate * sig
    slope = sig * (1.0 + act_gate * (1.0 - sig))
    hact = (swish * act_up).astype(BF16)
    dg32 = grad_act * act_up * slope
    du32 = grad_act * swish
    dg = dg32.astype(BF16)
    du = du32.astype(BF16)
    hact_ref[...] = hact
    dg_ref[...] = dg
    du_ref[...] = du
    dgi_ref[...] = (inv * dg32).astype(BF16)
    dui_ref[...] = (inv * du32).astype(BF16)
    probs = jnp.sum(hact.astype(F32) * grad_act, axis=1, keepdims=True)
    inner = jnp.sum(dg.astype(F32) * act_gate + du.astype(F32) * act_up, axis=1, keepdims=True)
    lane = lax.broadcasted_iota(jnp.int32, sc_ref.shape, 1)
    sc_ref[...] = jnp.where(
        lane == 0, probs, jnp.where(lane == 1, inner, jnp.where(lane == 2, inv, 0.0))
    )


def cot_kernel(core, own_ref, oth_ref, w_own_ref, w_oth_ref, ga_ref):
    ga_ref[...] = dot(own_ref[...], stacked(w_own_ref)) + dot(oth_ref[...], stacked(w_oth_ref))


def back_term(dg_ref, du_ref, wg_ref, wu_ref, block):
    return dot(dg_ref[...], wg_ref[block], ((1,), (1,))) + dot(
        du_ref[...], wu_ref[block], ((1,), (1,))
    )


def back_kernel(core, dg_ref, du_ref, wg_ref, wu_ref, out_ref):
    feat = wg_ref.shape[1]
    for block in range(wg_ref.shape[0]):
        term = back_term(dg_ref, du_ref, wg_ref, wu_ref, block)
        out_ref[:, block * feat : (block + 1) * feat] = term.astype(BF16)


def back_add_kernel(
    ctx_count, core, dg_ref, du_ref, wg_ref, wu_ref, other_ref, sc_ref, sc_other_ref, out_ref
):
    feat = wg_ref.shape[1]
    width = wg_ref.shape[0] * feat
    for block in range(wg_ref.shape[0]):
        lanes = slice(block * feat, (block + 1) * feat)
        term = back_term(dg_ref, du_ref, wg_ref, wu_ref, block).astype(BF16).astype(F32)
        out_ref[:, lanes] = (term + other_ref[:, lanes].astype(F32)).astype(BF16)
    small = sc_ref[...] + sc_other_ref[...]
    lane = lax.broadcasted_iota(jnp.int32, small.shape, 1)
    small = jnp.where(lane == 2, small * (0.5 / ctx_count), small)
    head = small.astype(BF16).astype(F32)
    tail = pltpu.roll(small - head, 3, 1)
    out_ref[:, width:] = jnp.where(lane < 3, head, jnp.where(lane < 6, tail, 0.0)).astype(BF16)


def grads_kernel(
    core, own_ref, oth_ref, cot_own_ref, cot_oth_ref, gown_ref, goth_ref, dgi_ref, dui_ref,
    hact_ref, gate_ref, up_ref, down_ref,
):
    here = core[0]
    first = ((0,), (0,))
    for rows_ref, cot_ref, gain_ref, place in (
        (own_ref, cot_own_ref, gown_ref, here),
        (oth_ref, cot_oth_ref, goth_ref, 1 - here),
    ):
        scaled = (rows_ref[...].astype(F32) * gain_ref[...]).astype(BF16)
        gate_ref[place] = dot(scaled, dgi_ref[...], first).astype(BF16)
        up_ref[place] = dot(scaled, dui_ref[...], first).astype(BF16)
        down_ref[place] = dot(cot_ref[...], hact_ref[...], first).astype(BF16)


def sums_kernel(got_ref, out_ref):
    feat = out_ref.shape[2] - 128
    count = out_ref.shape[0]

    def total(start, width):
        acc = got_ref[0, :, start : start + width].astype(F32)
        for block in range(1, got_ref.shape[0]):
            acc += got_ref[block, :, start : start + width].astype(F32)
        return acc

    small = total(count * feat, 128)
    lane = lax.broadcasted_iota(jnp.int32, small.shape, 1)
    small = jnp.where(lane < 3, small + pltpu.roll(small, 125, 1), 0.0)
    head = small.astype(BF16).astype(F32)
    small = (head + pltpu.roll(small - head, 3, 1)).astype(BF16)
    for block in range(count):
        out_ref[block, :, :feat] = total(block * feat, feat).astype(BF16)
        out_ref[block, :, feat:] = small


def whole(shape):
    return pl.BlockSpec(shape, lambda e, *_: (0,) * len(shape))


def side_by_side(blocks):
    return jnp.concatenate([blocks[e] for e in range(blocks.shape[0])], axis=1)


def per_device(
    residual,
    ssm_values,
    ssm_keys,
    ssm_queries,
    log_decay,
    expert_ids,
    gate_probs,
    norm_gain,
    w_gate,
    w_up,
    w_down,
    out_grad,
):
    tokens, feat = residual.shape
    heads = log_decay.shape[1]
    model_width, units = w_gate.shape[1:]
    ctx_count = lax.axis_size("ctx")
    exp_count = lax.axis_size("exp")
    capacity = 5 * tokens // (2 * exp_count)
    rows_all = ctx_count * capacity
    ctx_here = lax.axis_index("ctx")
    core = lax.axis_index("dp").astype(jnp.int32).reshape(1)
    other_core = [(0, 1), (1, 0)]

    values = ssm_values.astype(F32)
    key_rows = ssm_keys.astype(F32)
    queries = ssm_queries.astype(F32)
    (total_log, state_local), state_pull = jax.vjp(block_state, values, key_rows, log_decay)
    state_rows = state_local.shape[0]
    payload = jnp.concatenate(
        [state_local.astype(BF16), pad_rows(split_rows(total_log, 3), 8, feat)], axis=0
    )
    got = to_all(payload, "ctx")
    logs = jnp.sum(got[:, state_rows : state_rows + 3, :heads].astype(F32), axis=1)
    source = lax.broadcasted_iota(jnp.int32, (ctx_count, ctx_count), 0)
    between = lax.broadcasted_iota(jnp.int32, (ctx_count, ctx_count), 1)
    spread = head_map(heads, feat)
    rank = jnp.arange(ctx_count, dtype=jnp.int32)[:, None]
    before = ((between > source) & (between < ctx_here)).astype(F32)
    after = ((between < source) & (between > ctx_here)).astype(F32)
    gap_before = jnp.sum(before[:, :, None] * logs[None], axis=1)
    gap_after = jnp.sum(after[:, :, None] * logs[None], axis=1)
    weight_before = dot(
        jnp.where(rank < ctx_here, jnp.exp(gap_before), 0.0), spread, precision=HIGH
    )
    weight_after = dot(jnp.where(rank > ctx_here, jnp.exp(gap_after), 0.0), spread, precision=HIGH)
    state_in = jnp.sum(weight_before[:, None, :] * got[:, :state_rows].astype(F32), axis=0)

    ids = expert_ids.T
    probs = gate_probs.T
    experts = jnp.arange(exp_count, dtype=jnp.int32)[:, None]
    named = [ids[k][None, :] == experts for k in range(2)]
    member = named[0] | named[1]
    strict = (~lower_mask(tokens)).astype(BF16)
    order = dot(member.astype(BF16), strict).astype(jnp.int32)
    slot = lax.broadcasted_iota(jnp.int32, (exp_count, capacity, tokens), 1)
    chosen = (order[:, None, :] == slot) & member[:, None, :]
    select = chosen.astype(BF16).reshape(exp_count * capacity, tokens)
    select_each = jnp.concatenate(
        [
            (chosen & named[k][:, None, :]).astype(BF16).reshape(exp_count * capacity, tokens)
            for k in range(2)
        ],
        axis=1,
    )
    prob_of = jnp.where(named[0], probs[0][None, :], jnp.where(named[1], probs[1][None, :], 0.0))
    prob_rows = jnp.sum(jnp.where(chosen, prob_of[:, None, :], 0.0), axis=2)

    cot = (dot(select, out_grad).reshape(exp_count, capacity, feat) * prob_rows[:, :, None]).astype(
        BF16
    )
    mixer_out, output_pull = jax.vjp(
        block_output, values, key_rows, queries, log_decay, state_in
    )
    hidden = (residual.astype(F32) + mixer_out).astype(BF16)
    hidden_f = hidden.astype(F32)
    rows = dot(select, hidden).astype(BF16).reshape(exp_count, capacity, feat)
    gain_rows = pad_rows(split_rows(norm_gain[None, :], 3), 8, feat)
    gain_rows = jnp.broadcast_to(gain_rows[None], (exp_count,) + gain_rows.shape)
    got_rows = swap(jnp.concatenate([rows, cot, gain_rows], axis=1), "exp")
    gain_own = jnp.sum(got_rows[:, 2 * capacity : 2 * capacity + 3].astype(F32), axis=1)
    gain_oth = lax.ppermute(gain_own, "dp", other_core)
    gain4 = jnp.where(
        core[0] == 0,
        jnp.stack([gain_own, gain_oth], axis=1),
        jnp.stack([gain_oth, gain_own], axis=1),
    )
    gate4 = w_gate.reshape(exp_count, 2, feat, units)
    up4 = w_up.reshape(exp_count, 2, feat, units)
    down4 = w_down.reshape(exp_count, 2, feat, units)
    gate_scaled = (gate4.astype(F32) * gain4[:, :, :, None]).astype(BF16)
    up_scaled = (up4.astype(F32) * gain4[:, :, :, None]).astype(BF16)
    wide = exp_count * feat
    rows_all = ctx_count * capacity
    own = gather_rows(side_by_side(got_rows[:, :capacity])).reshape(rows_all, wide)
    cot_own = gather_cot(side_by_side(got_rows[:, capacity : 2 * capacity])).reshape(
        rows_all, wide
    )
    oth = lax.ppermute(own, "dp", other_core)
    cot_oth = lax.ppermute(cot_own, "dp", other_core)

    split = 2
    part = rows_all // split
    rows_spec = pl.BlockSpec((part, wide), lambda i, *_: (i, 0))
    acts = pl.BlockSpec((part, units), lambda i, *_: (i, 0))
    sums = pl.BlockSpec((part, 128), lambda i, *_: (i, 0))
    w_own = pl.BlockSpec((exp_count, None, feat, units), lambda i, s: (0, s[0], 0, 0))
    w_oth = pl.BlockSpec((exp_count, None, feat, units), lambda i, s: (0, 1 - s[0], 0, 0))
    acts_f = jax.ShapeDtypeStruct((rows_all, units), F32)
    acts_b = jax.ShapeDtypeStruct((rows_all, units), BF16)
    sums_f = jax.ShapeDtypeStruct((rows_all, 128), F32)

    def grid_of(n_scalars, steps, in_specs, out_specs):
        return pltpu.PrefetchScalarGridSpec(
            num_scalar_prefetch=n_scalars,
            grid=(steps,),
            in_specs=in_specs,
            out_specs=out_specs,
        )

    grad_act = pl.pallas_call(
        cot_kernel,
        grid_spec=grid_of(1, split, [rows_spec, rows_spec, w_own, w_oth], acts),
        out_shape=acts_f,
        name="cot",
    )(core, cot_own, cot_oth, down4, down4)
    ag, au, ss = pl.pallas_call(
        open_kernel,
        grid_spec=grid_of(1, split, [rows_spec, w_own, w_own], [acts, acts, sums]),
        out_shape=[acts_f, acts_f, sums_f],
        name="open",
    )(core, own, gate_scaled, up_scaled)
    hact, dg, du, dgi, dui, scal = pl.pallas_call(
        close_kernel,
        grid_spec=grid_of(
            1,
            split,
            [rows_spec, w_oth, w_oth, acts, acts, sums, acts],
            [acts] * 5 + [sums],
        ),
        out_shape=[acts_b] * 5 + [sums_f],
        name="close",
    )(core, oth, gate_scaled, up_scaled, ag, au, ss, grad_act)
    scal_got = lax.ppermute(scal, "dp", other_core)
    back_oth = pl.pallas_call(
        back_kernel,
        grid_spec=grid_of(1, split, [acts, acts, w_oth, w_oth], rows_spec),
        out_shape=jax.ShapeDtypeStruct((rows_all, wide), BF16),
        name="back_oth",
    )(core, dg, du, gate4, up4)
    back_got = lax.ppermute(back_oth, "dp", other_core)
    back = pl.pallas_call(
        functools.partial(back_add_kernel, ctx_count),
        grid_spec=grid_of(
            1,
            split,
            [acts, acts, w_own, w_own, rows_spec, sums, sums],
            pl.BlockSpec((part, wide + 128), lambda i, *_: (i, 0)),
        ),
        out_shape=jax.ShapeDtypeStruct((rows_all, wide + 128), BF16),
        name="back_own",
    )(core, dg, du, gate4, up4, back_got, scal, scal_got)
    columns = pl.BlockSpec((rows_all, feat), lambda e, *_: (0, e))
    gain_spec = pl.BlockSpec((None, 1, feat), lambda e, *_: (e, 0, 0))
    w_pair = pl.BlockSpec((None, 2, feat, units), lambda e, *_: (e, 0, 0, 0))
    acts_all = whole((rows_all, units))
    gate_grad, up_grad, down_grad = pl.pallas_call(
        grads_kernel,
        grid_spec=grid_of(
            1,
            exp_count,
            [
                columns,
                columns,
                columns,
                columns,
                gain_spec,
                gain_spec,
                acts_all,
                acts_all,
                acts_all,
            ],
            [w_pair] * 3,
        ),
        out_shape=[jax.ShapeDtypeStruct(gate4.shape, BF16)] * 3,
        name="grads",
    )(
        core, own, oth, cot_own, cot_oth, gain_own[:, None], gain_oth[:, None], dgi, dui, hact
    )

    got_sums = swap(back.reshape(ctx_count, capacity, wide + 128), "ctx")
    summed = pl.pallas_call(
        sums_kernel,
        out_shape=jax.ShapeDtypeStruct((exp_count, capacity, feat + 128), BF16),
        name="sums",
    )(got_sums)
    got_back = swap(summed, "exp").reshape(exp_count * capacity, feat + 128)
    grad_normed = dot(select, got_back[:, :feat], ((0,), (0,)))
    small = dot(select_each, got_back[:, feat:], ((0,), (0,)))
    small = small[:, :3] + small[:, 3:6]
    grad_probs = (
        jnp.concatenate([small[:tokens, :1], small[tokens:, :1]], axis=1) / gate_probs
    )
    inner = small[:tokens, 1:2] + small[tokens:, 1:2]
    inv_rms = small[:tokens, 2:3]
    scaled = grad_normed * norm_gain[None, :]
    grad_hidden = (
        out_grad.astype(F32)
        + inv_rms * scaled
        - hidden_f * (inv_rms * inv_rms * inner / model_width)
    )
    gain_part = jnp.sum(grad_normed * hidden_f * inv_rms, axis=0, keepdims=True)

    vals_first, keys_first, queries_part, decay_first, carry_cot = output_pull(grad_hidden)
    got_carry = to_all(
        jnp.concatenate(
            [carry_cot.astype(BF16), pad_rows(split_rows(gain_part, 3), 8, feat)], axis=0
        ),
        "ctx",
    )
    grad_state = jnp.sum(weight_after[:, None, :] * got_carry[:, :state_rows].astype(F32), axis=0)
    grad_gain = jnp.sum(got_carry[:, state_rows : state_rows + 3].astype(F32), axis=(0, 1))
    grad_total = dot(
        jnp.sum(grad_state * state_in, axis=0, keepdims=True), spread, ((1,), (1,)), HIGH
    ) * jnp.exp(total_log)
    vals_second, keys_second, decay_second = state_pull((grad_total, grad_state))
    both = jnp.concatenate([keys_first + keys_second, queries_part], axis=1).astype(BF16)
    both = (both.astype(F32) + lax.ppermute(both, "dp", other_core).astype(F32)).astype(BF16)
    both = jnp.sum(to_all(both, "exp").astype(F32), axis=0)
    return (
        grad_hidden.astype(BF16),
        (vals_first + vals_second).astype(BF16),
        both[:, :state_rows],
        both[:, state_rows:],
        decay_first + decay_second,
        grad_probs,
        grad_gain,
        gate_grad.reshape(w_gate.shape),
        up_grad.reshape(w_up.shape),
        down_grad.reshape(w_down.shape),
    )


def solution(mesh):
    rows = P("ctx", ("exp", "dp"))
    weights = P("exp", None, ("ctx", "dp"))
    ctx = P("ctx", None)
    gain = P(("exp", "dp"))
    return jax.shard_map(
        per_device,
        mesh=mesh,
        in_specs=(
            rows, rows, ctx, ctx, rows, ctx, ctx, gain, weights, weights, weights, rows,
        ),
        out_specs=(rows, rows, ctx, ctx, rows, ctx, gain, weights, weights, weights),
        check_vma=False,
    )
```

```python
import functools

import jax
import jax.numpy as jnp
from jax import lax
from jax.experimental import pallas as pl
from jax.experimental.pallas import tpu as pltpu
from jax.sharding import PartitionSpec as P


HIGH = lax.Precision.HIGHEST
EPS = 1e-05
F32 = jnp.float32
BF16 = jnp.bfloat16


def dot(a, b, dims=((1,), (0,)), precision=None):
    return lax.dot_general(a, b, (dims, ((), ())), precision=precision, preferred_element_type=F32)


def head_map(heads, width):
    size = width // heads
    return (
        lax.broadcasted_iota(jnp.int32, (heads, width), 1) // size
        == lax.broadcasted_iota(jnp.int32, (heads, width), 0)
    ).astype(F32)


def lower_mask(n):
    return lax.broadcasted_iota(jnp.int32, (n, n), 0) >= lax.broadcasted_iota(jnp.int32, (n, n), 1)


def block_state(values, key_rows, log_decay):
    tri = lower_mask(values.shape[0]).astype(F32)
    spread = head_map(log_decay.shape[1], values.shape[1])
    cumulative = dot(tri, log_decay, precision=HIGH)
    total_log = cumulative[-1:]
    tail = dot(jnp.exp(total_log - cumulative), spread, precision=HIGH)
    return total_log, dot(key_rows, tail * values, ((0,), (0,)), HIGH)


def block_output(values, key_rows, queries, log_decay, state_in):
    length, width = values.shape
    heads = log_decay.shape[1]
    size = width // heads
    causal = lower_mask(length)
    tri = causal.astype(F32)
    cumulative = dot(tri, log_decay, precision=HIGH)
    cum_heads = dot(log_decay, tri, ((0,), (1,)), HIGH)
    scores = dot(queries, key_rows, ((1,), (1,)), HIGH)
    parts = []
    for h in range(heads):
        log_gap = jnp.where(causal, cumulative[:, h : h + 1] - cum_heads[h : h + 1, :], 0.0)
        decay_mat = jnp.where(causal, jnp.exp(log_gap), 0.0)
        parts.append(dot(decay_mat * scores, values[:, h * size : (h + 1) * size], precision=HIGH))
    carried = dot(queries, state_in, precision=HIGH)
    growth = dot(jnp.exp(cumulative), head_map(heads, width), precision=HIGH)
    return jnp.concatenate(parts, axis=1) + growth * carried


def split_rows(x, parts):
    rows = []
    for _ in range(parts):
        head = lax.reduce_precision(x, 8, 7)
        rows.append(head.astype(BF16))
        x = x - head
    return rows


def pad_rows(rows, count, width):
    block = jnp.concatenate(rows, axis=0)
    return jnp.pad(block, ((0, count - block.shape[0]), (0, width - block.shape[1])))


def swap(x, axis):
    return lax.all_to_all(x, axis, 0, 0, tiled=True)


def to_all(x, axis):
    return swap(jnp.broadcast_to(x[None], (lax.axis_size(axis),) + x.shape), axis)


SIDE = 4


def along_y(step):
    return [
        (y * SIDE + x, (y + step) % SIDE * SIDE + x) for y in range(SIDE) for x in range(SIDE)
    ]


def along_x(step):
    return [
        (y * SIDE + x, y * SIDE + (x + step) % SIDE) for y in range(SIDE) for x in range(SIDE)
    ]


def gather_rows(block):
    def spread(x, groups):
        return lax.all_to_all(
            jnp.broadcast_to(x[None], (SIDE,) + x.shape),
            "ctx",
            0,
            0,
            tiled=True,
            axis_index_groups=groups,
        )

    row = spread(block, [[y * SIDE + x for x in range(SIDE)] for y in range(SIDE)])
    return spread(row, [[y * SIDE + x for y in range(SIDE)] for x in range(SIDE)])


def gather_cot(block):
    here = lax.axis_index("ctx")
    y, x = here // SIDE, here % SIDE
    put = lax.dynamic_update_slice
    above = [lax.ppermute(block, "ctx", along_y(step)) for step in (1, 2, 3)]
    column = jnp.broadcast_to(block[None], (SIDE,) + block.shape)
    for step, piece in zip((1, 2, 3), above):
        column = put(column, piece[None], ((y + SIDE - step) % SIDE, 0, 0))
    left = lax.ppermute(column, "ctx", along_x(1))
    right = lax.ppermute(column, "ctx", along_x(3))
    half = SIDE // 2
    far_low = lax.ppermute(left[:half], "ctx", along_x(1))
    far_high = lax.ppermute(right[half:], "ctx", along_x(3))
    full = jnp.broadcast_to(column[:, None], (SIDE,) + column.shape)
    full = put(full, left[:, None], (0, (x + 3) % SIDE, 0, 0))
    full = put(full, right[:, None], (0, (x + 1) % SIDE, 0, 0))
    full = put(full, far_low[:, None], (0, (x + 2) % SIDE, 0, 0))
    return put(full, far_high[:, None], (half, (x + 2) % SIDE, 0, 0))


def sum_low(blocks):
    groups_y = [[y * SIDE + x for y in range(SIDE)] for x in range(SIDE)]
    groups_x = [[y * SIDE + x for x in range(SIDE)] for y in range(SIDE)]
    got = lax.all_to_all(blocks, "ctx", 0, 0, tiled=True, axis_index_groups=groups_y)
    part = jnp.sum(got.astype(F32), axis=0).astype(BF16)
    return lax.all_to_all(part, "ctx", 0, 0, tiled=True, axis_index_groups=groups_x)


def sum_high(blocks):
    here = lax.axis_index("ctx")
    y, x = here // SIDE, here % SIDE
    half = SIDE // 2

    def column(step, start=0, count=SIDE):
        piece = lax.dynamic_slice(
            blocks, (start, (x + step) % SIDE, 0, 0), (count, 1) + blocks.shape[2:]
        )
        return piece[:, 0]

    def added(a, b):
        return (a.astype(F32) + b.astype(F32)).astype(BF16)

    low = lax.ppermute(column(2, 0, half), "ctx", along_x(1))
    high = lax.ppermute(column(2, half, half), "ctx", along_x(3))
    right = jnp.concatenate([added(column(1, 0, half), low), column(1, half, half)])
    left = jnp.concatenate([column(3, 0, half), added(column(3, half, half), high)])
    got_left = lax.ppermute(right, "ctx", along_x(1))
    got_right = lax.ppermute(left, "ctx", along_x(3))
    part = column(0).astype(F32) + got_left.astype(F32) + got_right.astype(F32)
    part = part.astype(BF16)
    pieces = [
        lax.dynamic_index_in_dim(part, (y + step) % SIDE, 0, keepdims=False)
        for step in range(SIDE)
    ]
    return pieces[:1] + [
        lax.ppermute(pieces[step], "ctx", along_y(step)) for step in (1, 2, 3)
    ]


def stacked(ref):
    return ref[...].reshape(ref.shape[0] * ref.shape[1], ref.shape[2])


def square_sums(rows_ref, like):
    total = None
    for start in range(0, rows_ref.shape[1], like.shape[1]):
        part = rows_ref[:, start : start + like.shape[1]].astype(F32)
        total = part * part if total is None else total + part * part
    return jnp.broadcast_to(jnp.sum(total, axis=1, keepdims=True), like.shape)


def open_kernel(core, rows_ref, wg_ref, wu_ref, ag_ref, au_ref, ss_ref):
    ag_ref[...] = dot(rows_ref[...], stacked(wg_ref))
    au_ref[...] = dot(rows_ref[...], stacked(wu_ref))
    ss_ref[...] = square_sums(rows_ref, ss_ref)


def close_kernel(
    core, rows_ref, wg_ref, wu_ref, ag_in, au_in, ss_in, ga_ref,
    hact_ref, dg_ref, du_ref, dgi_ref, dui_ref, sc_ref,
):
    width = 2 * rows_ref.shape[1]
    total = (ss_in[...] + square_sums(rows_ref, ss_in))[:, :1]
    inv = lax.rsqrt(total / width + EPS)
    act_gate = inv * (ag_in[...] + dot(rows_ref[...], stacked(wg_ref)))
    act_up = inv * (au_in[...] + dot(rows_ref[...], stacked(wu_ref)))
    grad_act = ga_ref[...]
    sig = jax.nn.sigmoid(act_gate)
    swish = act_gate * sig
    slope = sig * (1.0 + act_gate * (1.0 - sig))
    hact = (swish * act_up).astype(BF16)
    dg32 = grad_act * act_up * slope
    du32 = grad_act * swish
    dg = dg32.astype(BF16)
    du = du32.astype(BF16)
    hact_ref[...] = hact
    dg_ref[...] = dg
    du_ref[...] = du
    dgi_ref[...] = (inv * dg32).astype(BF16)
    dui_ref[...] = (inv * du32).astype(BF16)
    probs = jnp.sum(hact.astype(F32) * grad_act, axis=1, keepdims=True)
    inner = jnp.sum(dg.astype(F32) * act_gate + du.astype(F32) * act_up, axis=1, keepdims=True)
    lane = lax.broadcasted_iota(jnp.int32, sc_ref.shape, 1)
    sc_ref[...] = jnp.where(
        lane == 0, probs, jnp.where(lane == 1, inner, jnp.where(lane == 2, inv, 0.0))
    )


def near_kernel(core, rows_ref, w_ref, ga_ref):
    ga_ref[...] = dot(rows_ref[...], stacked(w_ref))


def far_kernel(core, rows_ref, w_ref, ga_in, ga_ref):
    ga_ref[...] = ga_in[...] + dot(rows_ref[...], stacked(w_ref))


def back_term(dg_ref, du_ref, wg_ref, wu_ref, block):
    return dot(dg_ref[...], wg_ref[block], ((1,), (1,))) + dot(
        du_ref[...], wu_ref[block], ((1,), (1,))
    )


def back_kernel(core, dg_ref, du_ref, wg_ref, wu_ref, out_ref):
    feat = wg_ref.shape[1]
    for block in range(wg_ref.shape[0]):
        term = back_term(dg_ref, du_ref, wg_ref, wu_ref, block)
        out_ref[:, block * feat : (block + 1) * feat] = term.astype(BF16)


def back_add_kernel(
    ctx_count, core, dg_ref, du_ref, wg_ref, wu_ref, other_ref, sc_ref, sc_other_ref,
    low_ref, high_ref,
):
    feat = wg_ref.shape[1]
    width = wg_ref.shape[0] // 2 * feat
    for block in range(wg_ref.shape[0]):
        lanes = slice(block * feat, (block + 1) * feat)
        term = back_term(dg_ref, du_ref, wg_ref, wu_ref, block).astype(BF16).astype(F32)
        both = (term + other_ref[:, lanes].astype(F32)).astype(BF16)
        if block * feat < width:
            low_ref[:, lanes] = both
        else:
            high_ref[:, block * feat - width : (block + 1) * feat - width] = both
    small = sc_ref[...] + sc_other_ref[...]
    lane = lax.broadcasted_iota(jnp.int32, small.shape, 1)
    small = jnp.where(lane == 2, small * (0.5 / ctx_count), small)
    head = small.astype(BF16).astype(F32)
    tail = pltpu.roll(small - head, 3, 1)
    low_ref[:, width:] = jnp.where(lane < 3, head, jnp.where(lane < 6, tail, 0.0)).astype(BF16)


def scaled_grads_kernel(core, own_ref, oth_ref, gown_ref, goth_ref, act_ref, out_ref):
    here = core[0]
    for rows_ref, gain_ref, place in ((own_ref, gown_ref, here), (oth_ref, goth_ref, 1 - here)):
        scaled = (rows_ref[...].astype(F32) * gain_ref[...]).astype(BF16)
        out_ref[place] = dot(scaled, act_ref[...], ((0,), (0,))).astype(BF16)


def plain_grads_kernel(core, own_ref, oth_ref, act_ref, out_ref):
    here = core[0]
    out_ref[here] = dot(own_ref[...], act_ref[...], ((0,), (0,))).astype(BF16)
    out_ref[1 - here] = dot(oth_ref[...], act_ref[...], ((0,), (0,))).astype(BF16)


def sums_kernel(low_ref, h0_ref, h1_ref, h2_ref, h3_ref, out_ref):
    feat = out_ref.shape[2] - 128
    count = out_ref.shape[0] // 2

    def total(start, width):
        acc = low_ref[0, :, start : start + width].astype(F32)
        for block in range(1, low_ref.shape[0]):
            acc += low_ref[block, :, start : start + width].astype(F32)
        return acc

    small = total(count * feat, 128)
    lane = lax.broadcasted_iota(jnp.int32, small.shape, 1)
    small = jnp.where(lane < 3, small + pltpu.roll(small, 125, 1), 0.0)
    head = small.astype(BF16).astype(F32)
    small = (head + pltpu.roll(small - head, 3, 1)).astype(BF16)
    for block in range(count):
        out_ref[block, :, :feat] = total(block * feat, feat).astype(BF16)
        out_ref[block, :, feat:] = small
        lanes = slice(block * feat, (block + 1) * feat)
        high = h0_ref[:, lanes].astype(F32)
        for ref in (h1_ref, h2_ref, h3_ref):
            high += ref[:, lanes].astype(F32)
        out_ref[count + block, :, :feat] = high.astype(BF16)
        out_ref[count + block, :, feat:] = small


def whole(shape):
    return pl.BlockSpec(shape, lambda e, *_: (0,) * len(shape))


def side_by_side(blocks):
    return jnp.concatenate([blocks[e] for e in range(blocks.shape[0])], axis=1)


def per_device(
    residual,
    ssm_values,
    ssm_keys,
    ssm_queries,
    log_decay,
    expert_ids,
    gate_probs,
    norm_gain,
    w_gate,
    w_up,
    w_down,
    out_grad,
):
    tokens, feat = residual.shape
    heads = log_decay.shape[1]
    model_width, units = w_gate.shape[1:]
    ctx_count = lax.axis_size("ctx")
    exp_count = lax.axis_size("exp")
    capacity = 5 * tokens // (2 * exp_count)
    rows_all = ctx_count * capacity
    ctx_here = lax.axis_index("ctx")
    core = lax.axis_index("dp").astype(jnp.int32).reshape(1)
    other_core = [(0, 1), (1, 0)]

    values = ssm_values.astype(F32)
    key_rows = ssm_keys.astype(F32)
    queries = ssm_queries.astype(F32)
    (total_log, state_local), state_pull = jax.vjp(block_state, values, key_rows, log_decay)
    state_rows = state_local.shape[0]
    payload = jnp.concatenate(
        [state_local.astype(BF16), pad_rows(split_rows(total_log, 3), 8, feat)], axis=0
    )
    got = to_all(payload, "ctx")
    logs = jnp.sum(got[:, state_rows : state_rows + 3, :heads].astype(F32), axis=1)
    source = lax.broadcasted_iota(jnp.int32, (ctx_count, ctx_count), 0)
    between = lax.broadcasted_iota(jnp.int32, (ctx_count, ctx_count), 1)
    spread = head_map(heads, feat)
    rank = jnp.arange(ctx_count, dtype=jnp.int32)[:, None]
    before = ((between > source) & (between < ctx_here)).astype(F32)
    after = ((between < source) & (between > ctx_here)).astype(F32)
    gap_before = jnp.sum(before[:, :, None] * logs[None], axis=1)
    gap_after = jnp.sum(after[:, :, None] * logs[None], axis=1)
    weight_before = dot(
        jnp.where(rank < ctx_here, jnp.exp(gap_before), 0.0), spread, precision=HIGH
    )
    weight_after = dot(jnp.where(rank > ctx_here, jnp.exp(gap_after), 0.0), spread, precision=HIGH)
    state_in = jnp.sum(weight_before[:, None, :] * got[:, :state_rows].astype(F32), axis=0)

    ids = expert_ids.T
    probs = gate_probs.T
    experts = jnp.arange(exp_count, dtype=jnp.int32)[:, None]
    named = [ids[k][None, :] == experts for k in range(2)]
    member = named[0] | named[1]
    strict = (~lower_mask(tokens)).astype(BF16)
    order = dot(member.astype(BF16), strict).astype(jnp.int32)
    slot = lax.broadcasted_iota(jnp.int32, (exp_count, capacity, tokens), 1)
    chosen = (order[:, None, :] == slot) & member[:, None, :]
    select = chosen.astype(BF16).reshape(exp_count * capacity, tokens)
    select_each = jnp.concatenate(
        [
            (chosen & named[k][:, None, :]).astype(BF16).reshape(exp_count * capacity, tokens)
            for k in range(2)
        ],
        axis=1,
    )
    prob_of = jnp.where(named[0], probs[0][None, :], jnp.where(named[1], probs[1][None, :], 0.0))
    prob_rows = jnp.sum(jnp.where(chosen, prob_of[:, None, :], 0.0), axis=2)

    cot = (dot(select, out_grad).reshape(exp_count, capacity, feat) * prob_rows[:, :, None]).astype(
        BF16
    )
    mixer_out, output_pull = jax.vjp(
        block_output, values, key_rows, queries, log_decay, state_in
    )
    hidden = (residual.astype(F32) + mixer_out).astype(BF16)
    hidden_f = hidden.astype(F32)
    rows = dot(select, hidden).astype(BF16).reshape(exp_count, capacity, feat)
    gain_rows = pad_rows(split_rows(norm_gain[None, :], 3), 8, feat)
    gain_rows = jnp.broadcast_to(gain_rows[None], (exp_count,) + gain_rows.shape)
    got_rows = swap(jnp.concatenate([rows, cot, gain_rows], axis=1), "exp")
    gain_own = jnp.sum(got_rows[:, 2 * capacity : 2 * capacity + 3].astype(F32), axis=1)
    gain_oth = lax.ppermute(gain_own, "dp", other_core)
    gain4 = jnp.where(
        core[0] == 0,
        jnp.stack([gain_own, gain_oth], axis=1),
        jnp.stack([gain_oth, gain_own], axis=1),
    )
    gate4 = w_gate.reshape(exp_count, 2, feat, units)
    up4 = w_up.reshape(exp_count, 2, feat, units)
    down4 = w_down.reshape(exp_count, 2, feat, units)
    gate_scaled = (gate4.astype(F32) * gain4[:, :, :, None]).astype(BF16)
    up_scaled = (up4.astype(F32) * gain4[:, :, :, None]).astype(BF16)
    wide = exp_count * feat
    rows_all = ctx_count * capacity
    own = gather_rows(side_by_side(got_rows[:, :capacity])).reshape(rows_all, wide)
    cot_own = gather_cot(side_by_side(got_rows[:, capacity : 2 * capacity])).reshape(
        rows_all, wide
    )
    oth = lax.ppermute(own, "dp", other_core)
    cot_oth = lax.ppermute(cot_own, "dp", other_core)

    split = 2
    part = rows_all // split
    rows_spec = pl.BlockSpec((part, wide), lambda i, *_: (i, 0))
    acts = pl.BlockSpec((part, units), lambda i, *_: (i, 0))
    sums = pl.BlockSpec((part, 128), lambda i, *_: (i, 0))
    w_own = pl.BlockSpec((exp_count, None, feat, units), lambda i, s: (0, s[0], 0, 0))
    w_oth = pl.BlockSpec((exp_count, None, feat, units), lambda i, s: (0, 1 - s[0], 0, 0))
    acts_f = jax.ShapeDtypeStruct((rows_all, units), F32)
    acts_b = jax.ShapeDtypeStruct((rows_all, units), BF16)
    sums_f = jax.ShapeDtypeStruct((rows_all, 128), F32)

    def grid_of(n_scalars, steps, in_specs, out_specs):
        return pltpu.PrefetchScalarGridSpec(
            num_scalar_prefetch=n_scalars,
            grid=(steps,),
            in_specs=in_specs,
            out_specs=out_specs,
        )

    grad_act = pl.pallas_call(
        near_kernel,
        grid_spec=grid_of(1, split, [rows_spec, w_own], acts),
        out_shape=acts_f,
        name="cot_near",
    )(core, cot_own, down4)
    grad_act = pl.pallas_call(
        far_kernel,
        grid_spec=grid_of(1, split, [rows_spec, w_oth, acts], acts),
        out_shape=acts_f,
        name="cot_far",
    )(core, cot_oth, down4, grad_act)
    ag, au, ss = pl.pallas_call(
        open_kernel,
        grid_spec=grid_of(1, split, [rows_spec, w_own, w_own], [acts, acts, sums]),
        out_shape=[acts_f, acts_f, sums_f],
        name="open",
    )(core, own, gate_scaled, up_scaled)
    hact, dg, du, dgi, dui, scal = pl.pallas_call(
        close_kernel,
        grid_spec=grid_of(
            1,
            split,
            [rows_spec, w_oth, w_oth, acts, acts, sums, acts],
            [acts] * 5 + [sums],
        ),
        out_shape=[acts_b] * 5 + [sums_f],
        name="close",
    )(core, oth, gate_scaled, up_scaled, ag, au, ss, grad_act)
    scal_got = lax.ppermute(scal, "dp", other_core)
    back_oth = pl.pallas_call(
        back_kernel,
        grid_spec=grid_of(1, split, [acts, acts, w_oth, w_oth], rows_spec),
        out_shape=jax.ShapeDtypeStruct((rows_all, wide), BF16),
        name="back_oth",
    )(core, dg, du, gate4, up4)
    back_got = lax.ppermute(back_oth, "dp", other_core)
    narrow = wide // 2
    low, high = pl.pallas_call(
        functools.partial(back_add_kernel, ctx_count),
        grid_spec=grid_of(
            1,
            split,
            [acts, acts, w_own, w_own, rows_spec, sums, sums],
            [
                pl.BlockSpec((part, narrow + 128), lambda i, *_: (i, 0)),
                pl.BlockSpec((part, narrow), lambda i, *_: (i, 0)),
            ],
        ),
        out_shape=[
            jax.ShapeDtypeStruct((rows_all, narrow + 128), BF16),
            jax.ShapeDtypeStruct((rows_all, narrow), BF16),
        ],
        name="back_own",
    )(core, dg, du, gate4, up4, back_got, scal, scal_got)
    columns = pl.BlockSpec((rows_all, feat), lambda e, *_: (0, e))
    gain_spec = pl.BlockSpec((None, 1, feat), lambda e, *_: (e, 0, 0))
    w_pair = pl.BlockSpec((None, 2, feat, units), lambda e, *_: (e, 0, 0, 0))
    acts_all = whole((rows_all, units))
    grads_shape = jax.ShapeDtypeStruct(gate4.shape, BF16)

    def scaled_grads(act):
        return pl.pallas_call(
            scaled_grads_kernel,
            grid_spec=grid_of(
                1, exp_count, [columns, columns, gain_spec, gain_spec, acts_all], w_pair
            ),
            out_shape=grads_shape,
        )(core, own, oth, gain_own[:, None], gain_oth[:, None], act)

    gate_grad = scaled_grads(dgi)
    up_grad = scaled_grads(dui)
    down_grad = pl.pallas_call(
        plain_grads_kernel,
        grid_spec=grid_of(1, exp_count, [columns, columns, acts_all], w_pair),
        out_shape=grads_shape,
        name="down_grads",
    )(core, cot_own, cot_oth, hact)

    low = sum_low(low.reshape(SIDE, SIDE, capacity, narrow + 128))
    high = sum_high(high.reshape(SIDE, SIDE, capacity, narrow))
    summed = pl.pallas_call(
        sums_kernel,
        out_shape=jax.ShapeDtypeStruct((exp_count, capacity, feat + 128), BF16),
        name="sums",
    )(low, *high)
    got_back = swap(summed, "exp")
    got_back = got_back.reshape(exp_count * capacity, feat + 128)
    grad_normed = dot(select, got_back[:, :feat], ((0,), (0,)))
    small = dot(select_each, got_back[:, feat:], ((0,), (0,)))
    small = small[:, :3] + small[:, 3:6]
    grad_probs = (
        jnp.concatenate([small[:tokens, :1], small[tokens:, :1]], axis=1) / gate_probs
    )
    inner = small[:tokens, 1:2] + small[tokens:, 1:2]
    inv_rms = small[:tokens, 2:3]
    scaled = grad_normed * norm_gain[None, :]
    grad_hidden = (
        out_grad.astype(F32)
        + inv_rms * scaled
        - hidden_f * (inv_rms * inv_rms * inner / model_width)
    )
    gain_part = jnp.sum(grad_normed * hidden_f * inv_rms, axis=0, keepdims=True)

    vals_first, keys_first, queries_part, decay_first, carry_cot = output_pull(grad_hidden)
    got_carry = to_all(
        jnp.concatenate(
            [carry_cot.astype(BF16), pad_rows(split_rows(gain_part, 3), 8, feat)], axis=0
        ),
        "ctx",
    )
    grad_state = jnp.sum(weight_after[:, None, :] * got_carry[:, :state_rows].astype(F32), axis=0)
    grad_gain = jnp.sum(got_carry[:, state_rows : state_rows + 3].astype(F32), axis=(0, 1))
    grad_total = dot(
        jnp.sum(grad_state * state_in, axis=0, keepdims=True), spread, ((1,), (1,)), HIGH
    ) * jnp.exp(total_log)
    vals_second, keys_second, decay_second = state_pull((grad_total, grad_state))
    both = jnp.concatenate([keys_first + keys_second, queries_part], axis=1).astype(BF16)
    both = (both.astype(F32) + lax.ppermute(both, "dp", other_core).astype(F32)).astype(BF16)
    both = to_all(both, "exp")
    both = jnp.sum(both.astype(F32), axis=0)
    return (
        grad_hidden.astype(BF16),
        (vals_first + vals_second).astype(BF16),
        both[:, :state_rows],
        both[:, state_rows:],
        decay_first + decay_second,
        grad_probs,
        grad_gain,
        gate_grad.reshape(w_gate.shape),
        up_grad.reshape(w_up.shape),
        down_grad.reshape(w_down.shape),
    )


def solution(mesh):
    rows = P("ctx", ("exp", "dp"))
    weights = P("exp", None, ("ctx", "dp"))
    ctx = P("ctx", None)
    gain = P(("exp", "dp"))
    return jax.shard_map(
        per_device,
        mesh=mesh,
        in_specs=(
            rows, rows, ctx, ctx, rows, ctx, ctx, gain, weights, weights, weights, rows,
        ),
        out_specs=(rows, rows, ctx, ctx, rows, ctx, gain, weights, weights, weights),
        check_vma=False,
    )
```

```python
import functools

import jax
import jax.numpy as jnp
from jax import lax
from jax.experimental import pallas as pl
from jax.experimental.pallas import tpu as pltpu
from jax.sharding import PartitionSpec as P


HIGH = lax.Precision.HIGHEST
EPS = 1e-05
F32 = jnp.float32
BF16 = jnp.bfloat16


def dot(a, b, dims=((1,), (0,)), precision=None):
    return lax.dot_general(a, b, (dims, ((), ())), precision=precision, preferred_element_type=F32)


def head_map(heads, width):
    size = width // heads
    return (
        lax.broadcasted_iota(jnp.int32, (heads, width), 1) // size
        == lax.broadcasted_iota(jnp.int32, (heads, width), 0)
    ).astype(F32)


def lower_mask(n):
    return lax.broadcasted_iota(jnp.int32, (n, n), 0) >= lax.broadcasted_iota(jnp.int32, (n, n), 1)


def block_state(values, key_rows, log_decay):
    tri = lower_mask(values.shape[0]).astype(F32)
    spread = head_map(log_decay.shape[1], values.shape[1])
    cumulative = dot(tri, log_decay, precision=HIGH)
    total_log = cumulative[-1:]
    tail = dot(jnp.exp(total_log - cumulative), spread, precision=HIGH)
    return total_log, dot(key_rows, tail * values, ((0,), (0,)), HIGH)


def block_output(values, key_rows, queries, log_decay, state_in):
    length, width = values.shape
    heads = log_decay.shape[1]
    size = width // heads
    causal = lower_mask(length)
    tri = causal.astype(F32)
    cumulative = dot(tri, log_decay, precision=HIGH)
    cum_heads = dot(log_decay, tri, ((0,), (1,)), HIGH)
    scores = dot(queries, key_rows, ((1,), (1,)), HIGH)
    parts = []
    for h in range(heads):
        log_gap = jnp.where(causal, cumulative[:, h : h + 1] - cum_heads[h : h + 1, :], 0.0)
        decay_mat = jnp.where(causal, jnp.exp(log_gap), 0.0)
        parts.append(dot(decay_mat * scores, values[:, h * size : (h + 1) * size], precision=HIGH))
    carried = dot(queries, state_in, precision=HIGH)
    growth = dot(jnp.exp(cumulative), head_map(heads, width), precision=HIGH)
    return jnp.concatenate(parts, axis=1) + growth * carried


def split_rows(x, parts):
    rows = []
    for _ in range(parts):
        head = lax.reduce_precision(x, 8, 7)
        rows.append(head.astype(BF16))
        x = x - head
    return rows


def pad_rows(rows, count, width):
    block = jnp.concatenate(rows, axis=0)
    return jnp.pad(block, ((0, count - block.shape[0]), (0, width - block.shape[1])))


def swap(x, axis):
    return lax.all_to_all(x, axis, 0, 0, tiled=True)


def to_all(x, axis):
    return swap(jnp.broadcast_to(x[None], (lax.axis_size(axis),) + x.shape), axis)


SIDE = 4


def along_y(step):
    return [
        (y * SIDE + x, (y + step) % SIDE * SIDE + x) for y in range(SIDE) for x in range(SIDE)
    ]


def along_x(step):
    return [
        (y * SIDE + x, y * SIDE + (x + step) % SIDE) for y in range(SIDE) for x in range(SIDE)
    ]


def gather_rows(block):
    groups_x = [[y * SIDE + x for x in range(SIDE)] for y in range(SIDE)]
    groups_y = [[y * SIDE + x for y in range(SIDE)] for x in range(SIDE)]
    block = jnp.broadcast_to(block[None], (SIDE,) + block.shape)
    row = lax.all_to_all(block, "ctx", 0, 0, tiled=True, axis_index_groups=groups_x)
    row = jnp.broadcast_to(row[None], (SIDE,) + row.shape)
    return lax.all_to_all(row, "ctx", 0, 0, tiled=True, axis_index_groups=groups_y)


def gather_cot(block):
    here = lax.axis_index("ctx")
    y, x = here // SIDE, here % SIDE
    put = lax.dynamic_update_slice
    above = [lax.ppermute(block, "ctx", along_y(step)) for step in (1, 2, 3)]
    column = jnp.broadcast_to(block[None], (SIDE,) + block.shape)
    for step, piece in zip((1, 2, 3), above):
        column = put(column, piece[None], ((y + SIDE - step) % SIDE, 0, 0))
    left = lax.ppermute(column, "ctx", along_x(1))
    right = lax.ppermute(column, "ctx", along_x(3))
    half = SIDE // 2
    far_low = lax.ppermute(left[:half], "ctx", along_x(1))
    far_high = lax.ppermute(right[half:], "ctx", along_x(3))
    full = jnp.broadcast_to(column[:, None], (SIDE,) + column.shape)
    full = put(full, left[:, None], (0, (x + 3) % SIDE, 0, 0))
    full = put(full, right[:, None], (0, (x + 1) % SIDE, 0, 0))
    full = put(full, far_low[:, None], (0, (x + 2) % SIDE, 0, 0))
    return put(full, far_high[:, None], (half, (x + 2) % SIDE, 0, 0))


def sum_low(blocks):
    groups_y = [[y * SIDE + x for y in range(SIDE)] for x in range(SIDE)]
    groups_x = [[y * SIDE + x for x in range(SIDE)] for y in range(SIDE)]
    got = lax.all_to_all(blocks, "ctx", 0, 0, tiled=True, axis_index_groups=groups_y)
    part = jnp.sum(got.astype(F32), axis=0).astype(BF16)
    return lax.all_to_all(part, "ctx", 0, 0, tiled=True, axis_index_groups=groups_x)


def sum_high(blocks):
    here = lax.axis_index("ctx")
    y, x = here // SIDE, here % SIDE
    half = SIDE // 2

    def column(step, start=0, count=SIDE):
        piece = lax.dynamic_slice(
            blocks, (start, (x + step) % SIDE, 0, 0), (count, 1) + blocks.shape[2:]
        )
        return piece[:, 0]

    def added(a, b):
        return (a.astype(F32) + b.astype(F32)).astype(BF16)

    low = lax.ppermute(column(2, 0, half), "ctx", along_x(1))
    high = lax.ppermute(column(2, half, half), "ctx", along_x(3))
    right = jnp.concatenate([added(column(1, 0, half), low), column(1, half, half)])
    left = jnp.concatenate([column(3, 0, half), added(column(3, half, half), high)])
    got_left = lax.ppermute(right, "ctx", along_x(1))
    got_right = lax.ppermute(left, "ctx", along_x(3))
    part = column(0).astype(F32) + got_left.astype(F32) + got_right.astype(F32)
    part = part.astype(BF16)
    pieces = [
        lax.dynamic_index_in_dim(part, (y + step) % SIDE, 0, keepdims=False)
        for step in range(SIDE)
    ]
    return pieces[:1] + [
        lax.ppermute(pieces[step], "ctx", along_y(step)) for step in (1, 2, 3)
    ]


def stacked(ref):
    return ref[...].reshape(ref.shape[0] * ref.shape[1], ref.shape[2])


def square_sums(rows_ref, like):
    total = None
    for start in range(0, rows_ref.shape[1], like.shape[1]):
        part = rows_ref[:, start : start + like.shape[1]].astype(F32)
        total = part * part if total is None else total + part * part
    return jnp.broadcast_to(jnp.sum(total, axis=1, keepdims=True), like.shape)


def open_kernel(core, rows_ref, wg_ref, wu_ref, ag_ref, au_ref, ss_ref):
    ag_ref[...] = dot(rows_ref[...], stacked(wg_ref))
    au_ref[...] = dot(rows_ref[...], stacked(wu_ref))
    ss_ref[...] = square_sums(rows_ref, ss_ref)


def close_kernel(
    core, rows_ref, wg_ref, wu_ref, ag_in, au_in, ss_in, ga_ref,
    hact_ref, dg_ref, du_ref, dgi_ref, dui_ref, sc_ref,
):
    width = 2 * rows_ref.shape[1]
    total = (ss_in[...] + square_sums(rows_ref, ss_in))[:, :1]
    inv = lax.rsqrt(total / width + EPS)
    act_gate = inv * (ag_in[...] + dot(rows_ref[...], stacked(wg_ref)))
    act_up = inv * (au_in[...] + dot(rows_ref[...], stacked(wu_ref)))
    grad_act = ga_ref[...]
    sig = jax.nn.sigmoid(act_gate)
    swish = act_gate * sig
    slope = sig * (1.0 + act_gate * (1.0 - sig))
    hact = (swish * act_up).astype(BF16)
    dg32 = grad_act * act_up * slope
    du32 = grad_act * swish
    dg = dg32.astype(BF16)
    du = du32.astype(BF16)
    hact_ref[...] = hact
    dg_ref[...] = dg
    du_ref[...] = du
    dgi_ref[...] = (inv * dg32).astype(BF16)
    dui_ref[...] = (inv * du32).astype(BF16)
    probs = jnp.sum(hact.astype(F32) * grad_act, axis=1, keepdims=True)
    inner = jnp.sum(dg.astype(F32) * act_gate + du.astype(F32) * act_up, axis=1, keepdims=True)
    lane = lax.broadcasted_iota(jnp.int32, sc_ref.shape, 1)
    sc_ref[...] = jnp.where(
        lane == 0, probs, jnp.where(lane == 1, inner, jnp.where(lane == 2, inv, 0.0))
    )


def cot_kernel(core, own_ref, oth_ref, w_own_ref, w_oth_ref, ga_ref):
    ga_ref[...] = dot(own_ref[...], stacked(w_own_ref)) + dot(oth_ref[...], stacked(w_oth_ref))


def back_term(dg_ref, du_ref, wg_ref, wu_ref, block):
    return dot(dg_ref[...], wg_ref[block], ((1,), (1,))) + dot(
        du_ref[...], wu_ref[block], ((1,), (1,))
    )


def back_kernel(core, dg_ref, du_ref, wg_ref, wu_ref, out_ref):
    feat = wg_ref.shape[1]
    for block in range(wg_ref.shape[0]):
        term = back_term(dg_ref, du_ref, wg_ref, wu_ref, block)
        out_ref[:, block * feat : (block + 1) * feat] = term.astype(BF16)


def back_add_kernel(
    ctx_count, core, dg_ref, du_ref, wg_ref, wu_ref, other_ref, sc_ref, sc_other_ref,
    low_ref, high_ref,
):
    feat = wg_ref.shape[1]
    width = wg_ref.shape[0] // 2 * feat
    for block in range(wg_ref.shape[0]):
        lanes = slice(block * feat, (block + 1) * feat)
        term = back_term(dg_ref, du_ref, wg_ref, wu_ref, block).astype(BF16).astype(F32)
        both = (term + other_ref[:, lanes].astype(F32)).astype(BF16)
        if block * feat < width:
            low_ref[:, lanes] = both
        else:
            high_ref[:, block * feat - width : (block + 1) * feat - width] = both
    small = sc_ref[...] + sc_other_ref[...]
    lane = lax.broadcasted_iota(jnp.int32, small.shape, 1)
    small = jnp.where(lane == 2, small * (0.5 / ctx_count), small)
    head = small.astype(BF16).astype(F32)
    tail = pltpu.roll(small - head, 3, 1)
    low_ref[:, width:] = jnp.where(lane < 3, head, jnp.where(lane < 6, tail, 0.0)).astype(BF16)


def scaled_grads_kernel(
    core, own_ref, oth_ref, gown_ref, goth_ref, dgi_ref, dui_ref, gate_ref, up_ref
):
    here = core[0]
    for rows_ref, gain_ref, place in ((own_ref, gown_ref, here), (oth_ref, goth_ref, 1 - here)):
        scaled = (rows_ref[...].astype(F32) * gain_ref[...]).astype(BF16)
        gate_ref[place] = dot(scaled, dgi_ref[...], ((0,), (0,))).astype(BF16)
        up_ref[place] = dot(scaled, dui_ref[...], ((0,), (0,))).astype(BF16)


def plain_grads_kernel(core, own_ref, oth_ref, act_ref, out_ref):
    here = core[0]
    out_ref[here] = dot(own_ref[...], act_ref[...], ((0,), (0,))).astype(BF16)
    out_ref[1 - here] = dot(oth_ref[...], act_ref[...], ((0,), (0,))).astype(BF16)


def sums_kernel(low_ref, h0_ref, h1_ref, h2_ref, h3_ref, out_ref):
    feat = out_ref.shape[2] - 128
    count = out_ref.shape[0] // 2

    def total(start, width):
        acc = low_ref[0, :, start : start + width].astype(F32)
        for block in range(1, low_ref.shape[0]):
            acc += low_ref[block, :, start : start + width].astype(F32)
        return acc

    small = total(count * feat, 128)
    lane = lax.broadcasted_iota(jnp.int32, small.shape, 1)
    small = jnp.where(lane < 3, small + pltpu.roll(small, 125, 1), 0.0)
    head = small.astype(BF16).astype(F32)
    small = (head + pltpu.roll(small - head, 3, 1)).astype(BF16)
    for block in range(count):
        out_ref[block, :, :feat] = total(block * feat, feat).astype(BF16)
        out_ref[block, :, feat:] = small
        lanes = slice(block * feat, (block + 1) * feat)
        high = h0_ref[:, lanes].astype(F32)
        for ref in (h1_ref, h2_ref, h3_ref):
            high += ref[:, lanes].astype(F32)
        out_ref[count + block, :, :feat] = high.astype(BF16)
        out_ref[count + block, :, feat:] = small


def whole(shape):
    return pl.BlockSpec(shape, lambda e, *_: (0,) * len(shape))


def side_by_side(blocks):
    return jnp.concatenate([blocks[e] for e in range(blocks.shape[0])], axis=1)


def per_device(
    residual,
    ssm_values,
    ssm_keys,
    ssm_queries,
    log_decay,
    expert_ids,
    gate_probs,
    norm_gain,
    w_gate,
    w_up,
    w_down,
    out_grad,
):
    tokens, feat = residual.shape
    heads = log_decay.shape[1]
    model_width, units = w_gate.shape[1:]
    ctx_count = lax.axis_size("ctx")
    exp_count = lax.axis_size("exp")
    capacity = 5 * tokens // (2 * exp_count)
    rows_all = ctx_count * capacity
    ctx_here = lax.axis_index("ctx")
    core = lax.axis_index("dp").astype(jnp.int32).reshape(1)
    other_core = [(0, 1), (1, 0)]

    values = ssm_values.astype(F32)
    key_rows = ssm_keys.astype(F32)
    queries = ssm_queries.astype(F32)
    (total_log, state_local), state_pull = jax.vjp(block_state, values, key_rows, log_decay)
    state_rows = state_local.shape[0]
    payload = jnp.concatenate(
        [state_local.astype(BF16), pad_rows(split_rows(total_log, 3), 8, feat)], axis=0
    )
    got = to_all(payload, "ctx")
    logs = jnp.sum(got[:, state_rows : state_rows + 3, :heads].astype(F32), axis=1)
    source = lax.broadcasted_iota(jnp.int32, (ctx_count, ctx_count), 0)
    between = lax.broadcasted_iota(jnp.int32, (ctx_count, ctx_count), 1)
    spread = head_map(heads, feat)
    rank = jnp.arange(ctx_count, dtype=jnp.int32)[:, None]
    before = ((between > source) & (between < ctx_here)).astype(F32)
    after = ((between < source) & (between > ctx_here)).astype(F32)
    gap_before = jnp.sum(before[:, :, None] * logs[None], axis=1)
    gap_after = jnp.sum(after[:, :, None] * logs[None], axis=1)
    weight_before = dot(
        jnp.where(rank < ctx_here, jnp.exp(gap_before), 0.0), spread, precision=HIGH
    )
    weight_after = dot(jnp.where(rank > ctx_here, jnp.exp(gap_after), 0.0), spread, precision=HIGH)
    state_in = jnp.sum(weight_before[:, None, :] * got[:, :state_rows].astype(F32), axis=0)

    ids = expert_ids.T
    probs = gate_probs.T
    experts = jnp.arange(exp_count, dtype=jnp.int32)[:, None]
    named = [ids[k][None, :] == experts for k in range(2)]
    member = named[0] | named[1]
    strict = (~lower_mask(tokens)).astype(BF16)
    order = dot(member.astype(BF16), strict).astype(jnp.int32)
    slot = lax.broadcasted_iota(jnp.int32, (exp_count, capacity, tokens), 1)
    chosen = (order[:, None, :] == slot) & member[:, None, :]
    select = chosen.astype(BF16).reshape(exp_count * capacity, tokens)
    select_each = jnp.concatenate(
        [
            (chosen & named[k][:, None, :]).astype(BF16).reshape(exp_count * capacity, tokens)
            for k in range(2)
        ],
        axis=1,
    )
    prob_of = jnp.where(named[0], probs[0][None, :], jnp.where(named[1], probs[1][None, :], 0.0))
    prob_rows = jnp.sum(jnp.where(chosen, prob_of[:, None, :], 0.0), axis=2)

    cot = (dot(select, out_grad).reshape(exp_count, capacity, feat) * prob_rows[:, :, None]).astype(
        BF16
    )
    mixer_out, output_pull = jax.vjp(
        block_output, values, key_rows, queries, log_decay, state_in
    )
    hidden = (residual.astype(F32) + mixer_out).astype(BF16)
    hidden_f = hidden.astype(F32)
    rows = dot(select, hidden).astype(BF16).reshape(exp_count, capacity, feat)
    gain_rows = pad_rows(split_rows(norm_gain[None, :], 3), 8, feat)
    gain_rows = jnp.broadcast_to(gain_rows[None], (exp_count,) + gain_rows.shape)
    got_rows = swap(jnp.concatenate([rows, cot, gain_rows], axis=1), "exp")
    gain_own = jnp.sum(got_rows[:, 2 * capacity : 2 * capacity + 3].astype(F32), axis=1)
    gain_oth = lax.ppermute(gain_own, "dp", other_core)
    gain4 = jnp.where(
        core[0] == 0,
        jnp.stack([gain_own, gain_oth], axis=1),
        jnp.stack([gain_oth, gain_own], axis=1),
    )
    gate4 = w_gate.reshape(exp_count, 2, feat, units)
    up4 = w_up.reshape(exp_count, 2, feat, units)
    down4 = w_down.reshape(exp_count, 2, feat, units)
    gate_scaled = (gate4.astype(F32) * gain4[:, :, :, None]).astype(BF16)
    up_scaled = (up4.astype(F32) * gain4[:, :, :, None]).astype(BF16)
    wide = exp_count * feat
    rows_all = ctx_count * capacity
    own = gather_rows(side_by_side(got_rows[:, :capacity])).reshape(rows_all, wide)
    cot_own = gather_cot(side_by_side(got_rows[:, capacity : 2 * capacity])).reshape(
        rows_all, wide
    )
    oth = lax.ppermute(own, "dp", other_core)
    cot_oth = lax.ppermute(cot_own, "dp", other_core)

    split = 2
    part = rows_all // split
    rows_spec = pl.BlockSpec((part, wide), lambda i, *_: (i, 0))
    acts = pl.BlockSpec((part, units), lambda i, *_: (i, 0))
    sums = pl.BlockSpec((part, 128), lambda i, *_: (i, 0))
    w_own = pl.BlockSpec((exp_count, None, feat, units), lambda i, s: (0, s[0], 0, 0))
    w_oth = pl.BlockSpec((exp_count, None, feat, units), lambda i, s: (0, 1 - s[0], 0, 0))
    acts_f = jax.ShapeDtypeStruct((rows_all, units), F32)
    acts_b = jax.ShapeDtypeStruct((rows_all, units), BF16)
    sums_f = jax.ShapeDtypeStruct((rows_all, 128), F32)

    def grid_of(n_scalars, steps, in_specs, out_specs):
        return pltpu.PrefetchScalarGridSpec(
            num_scalar_prefetch=n_scalars,
            grid=(steps,),
            in_specs=in_specs,
            out_specs=out_specs,
        )

    grad_act = pl.pallas_call(
        cot_kernel,
        grid_spec=grid_of(1, split, [rows_spec, rows_spec, w_own, w_oth], acts),
        out_shape=acts_f,
        name="cot",
    )(core, cot_own, cot_oth, down4, down4)
    ag, au, ss = pl.pallas_call(
        open_kernel,
        grid_spec=grid_of(1, split, [rows_spec, w_own, w_own], [acts, acts, sums]),
        out_shape=[acts_f, acts_f, sums_f],
        name="open",
    )(core, own, gate_scaled, up_scaled)
    hact, dg, du, dgi, dui, scal = pl.pallas_call(
        close_kernel,
        grid_spec=grid_of(
            1,
            split,
            [rows_spec, w_oth, w_oth, acts, acts, sums, acts],
            [acts] * 5 + [sums],
        ),
        out_shape=[acts_b] * 5 + [sums_f],
        name="close",
    )(core, oth, gate_scaled, up_scaled, ag, au, ss, grad_act)
    scal_got = lax.ppermute(scal, "dp", other_core)
    back_oth = pl.pallas_call(
        back_kernel,
        grid_spec=grid_of(1, split, [acts, acts, w_oth, w_oth], rows_spec),
        out_shape=jax.ShapeDtypeStruct((rows_all, wide), BF16),
        name="back_oth",
    )(core, dg, du, gate4, up4)
    back_got = lax.ppermute(back_oth, "dp", other_core)
    narrow = wide // 2
    low, high = pl.pallas_call(
        functools.partial(back_add_kernel, ctx_count),
        grid_spec=grid_of(
            1,
            split,
            [acts, acts, w_own, w_own, rows_spec, sums, sums],
            [
                pl.BlockSpec((part, narrow + 128), lambda i, *_: (i, 0)),
                pl.BlockSpec((part, narrow), lambda i, *_: (i, 0)),
            ],
        ),
        out_shape=[
            jax.ShapeDtypeStruct((rows_all, narrow + 128), BF16),
            jax.ShapeDtypeStruct((rows_all, narrow), BF16),
        ],
        name="back_own",
    )(core, dg, du, gate4, up4, back_got, scal, scal_got)
    columns = pl.BlockSpec((rows_all, feat), lambda e, *_: (0, e))
    gain_spec = pl.BlockSpec((None, 1, feat), lambda e, *_: (e, 0, 0))
    w_pair = pl.BlockSpec((None, 2, feat, units), lambda e, *_: (e, 0, 0, 0))
    acts_all = whole((rows_all, units))
    grads_shape = jax.ShapeDtypeStruct(gate4.shape, BF16)

    gate_grad, up_grad = pl.pallas_call(
        scaled_grads_kernel,
        grid_spec=grid_of(
            1,
            exp_count,
            [columns, columns, gain_spec, gain_spec, acts_all, acts_all],
            [w_pair] * 2,
        ),
        out_shape=[grads_shape] * 2,
        name="gate_grads",
    )(core, own, oth, gain_own[:, None], gain_oth[:, None], dgi, dui)
    down_grad = pl.pallas_call(
        plain_grads_kernel,
        grid_spec=grid_of(1, exp_count, [columns, columns, acts_all], w_pair),
        out_shape=grads_shape,
        name="down_grads",
    )(core, cot_own, cot_oth, hact)

    low = sum_low(low.reshape(SIDE, SIDE, capacity, narrow + 128))
    high = sum_high(high.reshape(SIDE, SIDE, capacity, narrow))
    summed = pl.pallas_call(
        sums_kernel,
        out_shape=jax.ShapeDtypeStruct((exp_count, capacity, feat + 128), BF16),
        name="sums",
    )(low, *high)
    got_back = swap(summed, "exp")
    got_back = got_back.reshape(exp_count * capacity, feat + 128)
    grad_normed = dot(select, got_back[:, :feat], ((0,), (0,)))
    small = dot(select_each, got_back[:, feat:], ((0,), (0,)))
    small = small[:, :3] + small[:, 3:6]
    grad_probs = (
        jnp.concatenate([small[:tokens, :1], small[tokens:, :1]], axis=1) / gate_probs
    )
    inner = small[:tokens, 1:2] + small[tokens:, 1:2]
    inv_rms = small[:tokens, 2:3]
    scaled = grad_normed * norm_gain[None, :]
    grad_hidden = (
        out_grad.astype(F32)
        + inv_rms * scaled
        - hidden_f * (inv_rms * inv_rms * inner / model_width)
    )
    gain_part = jnp.sum(grad_normed * hidden_f * inv_rms, axis=0, keepdims=True)

    vals_first, keys_first, queries_part, decay_first, carry_cot = output_pull(grad_hidden)
    got_carry = to_all(
        jnp.concatenate(
            [carry_cot.astype(BF16), pad_rows(split_rows(gain_part, 3), 8, feat)], axis=0
        ),
        "ctx",
    )
    grad_state = jnp.sum(weight_after[:, None, :] * got_carry[:, :state_rows].astype(F32), axis=0)
    grad_gain = jnp.sum(got_carry[:, state_rows : state_rows + 3].astype(F32), axis=(0, 1))
    grad_total = dot(
        jnp.sum(grad_state * state_in, axis=0, keepdims=True), spread, ((1,), (1,)), HIGH
    ) * jnp.exp(total_log)
    vals_second, keys_second, decay_second = state_pull((grad_total, grad_state))
    both = jnp.concatenate([keys_first + keys_second, queries_part], axis=1).astype(BF16)
    both = (both.astype(F32) + lax.ppermute(both, "dp", other_core).astype(F32)).astype(BF16)
    both = to_all(both, "exp")
    keys_grad = jnp.sum(both[:, :, :state_rows].astype(F32), axis=0)
    queries_grad = jnp.sum(both[:, :, state_rows:].astype(F32), axis=0)
    return (
        grad_hidden.astype(BF16),
        (vals_first + vals_second).astype(BF16),
        keys_grad,
        queries_grad,
        decay_first + decay_second,
        grad_probs,
        grad_gain,
        gate_grad.reshape(w_gate.shape),
        up_grad.reshape(w_up.shape),
        down_grad.reshape(w_down.shape),
    )


def solution(mesh):
    rows = P("ctx", ("exp", "dp"))
    weights = P("exp", None, ("ctx", "dp"))
    ctx = P("ctx", None)
    gain = P(("exp", "dp"))
    return jax.shard_map(
        per_device,
        mesh=mesh,
        in_specs=(
            rows, rows, ctx, ctx, rows, ctx, ctx, gain, weights, weights, weights, rows,
        ),
        out_specs=(rows, rows, ctx, ctx, rows, ctx, gain, weights, weights, weights),
        check_vma=False,
    )
```

```python
import functools

import jax
import jax.numpy as jnp
from jax import lax
from jax.experimental import pallas as pl
from jax.experimental.pallas import tpu as pltpu
from jax.sharding import PartitionSpec as P


HIGH = lax.Precision.HIGHEST
EPS = 1e-05
F32 = jnp.float32
BF16 = jnp.bfloat16


def dot(a, b, dims=((1,), (0,)), precision=None):
    return lax.dot_general(a, b, (dims, ((), ())), precision=precision, preferred_element_type=F32)


def head_map(heads, width):
    size = width // heads
    return (
        lax.broadcasted_iota(jnp.int32, (heads, width), 1) // size
        == lax.broadcasted_iota(jnp.int32, (heads, width), 0)
    ).astype(F32)


def lower_mask(n):
    return lax.broadcasted_iota(jnp.int32, (n, n), 0) >= lax.broadcasted_iota(jnp.int32, (n, n), 1)


def block_state(values, key_rows, log_decay):
    tri = lower_mask(values.shape[0]).astype(F32)
    spread = head_map(log_decay.shape[1], values.shape[1])
    cumulative = dot(tri, log_decay, precision=HIGH)
    total_log = cumulative[-1:]
    tail = dot(jnp.exp(total_log - cumulative), spread, precision=HIGH)
    return total_log, dot(key_rows, tail * values, ((0,), (0,)), HIGH)


def block_output(values, key_rows, queries, log_decay, state_in):
    length, width = values.shape
    heads = log_decay.shape[1]
    size = width // heads
    causal = lower_mask(length)
    tri = causal.astype(F32)
    cumulative = dot(tri, log_decay, precision=HIGH)
    cum_heads = dot(log_decay, tri, ((0,), (1,)), HIGH)
    scores = dot(queries, key_rows, ((1,), (1,)), HIGH)
    parts = []
    for h in range(heads):
        log_gap = jnp.where(causal, cumulative[:, h : h + 1] - cum_heads[h : h + 1, :], 0.0)
        decay_mat = jnp.where(causal, jnp.exp(log_gap), 0.0)
        parts.append(dot(decay_mat * scores, values[:, h * size : (h + 1) * size], precision=HIGH))
    carried = dot(queries, state_in, precision=HIGH)
    growth = dot(jnp.exp(cumulative), head_map(heads, width), precision=HIGH)
    return jnp.concatenate(parts, axis=1) + growth * carried


def split_rows(x, parts):
    rows = []
    for _ in range(parts):
        head = lax.reduce_precision(x, 8, 7)
        rows.append(head.astype(BF16))
        x = x - head
    return rows


def pad_rows(rows, count, width):
    block = jnp.concatenate(rows, axis=0)
    return jnp.pad(block, ((0, count - block.shape[0]), (0, width - block.shape[1])))


def swap(x, axis):
    return lax.all_to_all(x, axis, 0, 0, tiled=True)


def to_all(x, axis):
    return swap(jnp.broadcast_to(x[None], (lax.axis_size(axis),) + x.shape), axis)


SIDE = 4


def along_y(step):
    return [
        (y * SIDE + x, (y + step) % SIDE * SIDE + x) for y in range(SIDE) for x in range(SIDE)
    ]


def along_x(step):
    return [
        (y * SIDE + x, y * SIDE + (x + step) % SIDE) for y in range(SIDE) for x in range(SIDE)
    ]


def gather_rows(block):
    groups_x = [[y * SIDE + x for x in range(SIDE)] for y in range(SIDE)]
    groups_y = [[y * SIDE + x for y in range(SIDE)] for x in range(SIDE)]
    block = jnp.broadcast_to(block[None], (SIDE,) + block.shape)
    row = lax.all_to_all(block, "ctx", 0, 0, tiled=True, axis_index_groups=groups_x)
    row = jnp.broadcast_to(row[None], (SIDE,) + row.shape)
    return lax.all_to_all(row, "ctx", 0, 0, tiled=True, axis_index_groups=groups_y)


def gather_cot(block):
    here = lax.axis_index("ctx")
    y, x = here // SIDE, here % SIDE
    put = lax.dynamic_update_slice
    above = [lax.ppermute(block, "ctx", along_y(step)) for step in (1, 2, 3)]
    column = jnp.broadcast_to(block[None], (SIDE,) + block.shape)
    for step, piece in zip((1, 2, 3), above):
        column = put(column, piece[None], ((y + SIDE - step) % SIDE, 0, 0))
    left = lax.ppermute(column, "ctx", along_x(1))
    right = lax.ppermute(column, "ctx", along_x(3))
    half = SIDE // 2
    far_low = lax.ppermute(left[:half], "ctx", along_x(1))
    far_high = lax.ppermute(right[half:], "ctx", along_x(3))
    full = jnp.broadcast_to(column[:, None], (SIDE,) + column.shape)
    full = put(full, left[:, None], (0, (x + 3) % SIDE, 0, 0))
    full = put(full, right[:, None], (0, (x + 1) % SIDE, 0, 0))
    full = put(full, far_low[:, None], (0, (x + 2) % SIDE, 0, 0))
    return put(full, far_high[:, None], (half, (x + 2) % SIDE, 0, 0))


def sum_low(blocks):
    groups_y = [[y * SIDE + x for y in range(SIDE)] for x in range(SIDE)]
    groups_x = [[y * SIDE + x for x in range(SIDE)] for y in range(SIDE)]
    got = lax.all_to_all(blocks, "ctx", 0, 0, tiled=True, axis_index_groups=groups_y)
    part = jnp.sum(got.astype(F32), axis=0).astype(BF16)
    return lax.all_to_all(part, "ctx", 0, 0, tiled=True, axis_index_groups=groups_x)


def sum_high(blocks):
    here = lax.axis_index("ctx")
    y, x = here // SIDE, here % SIDE
    half = SIDE // 2

    def column(step, start=0, count=SIDE):
        piece = lax.dynamic_slice(
            blocks, (start, (x + step) % SIDE, 0, 0), (count, 1) + blocks.shape[2:]
        )
        return piece[:, 0]

    def added(a, b):
        return (a.astype(F32) + b.astype(F32)).astype(BF16)

    low = lax.ppermute(column(2, 0, half), "ctx", along_x(1))
    high = lax.ppermute(column(2, half, half), "ctx", along_x(3))
    right = jnp.concatenate([added(column(1, 0, half), low), column(1, half, half)])
    left = jnp.concatenate([column(3, 0, half), added(column(3, half, half), high)])
    got_left = lax.ppermute(right, "ctx", along_x(1))
    got_right = lax.ppermute(left, "ctx", along_x(3))
    part = column(0).astype(F32) + got_left.astype(F32) + got_right.astype(F32)
    part = part.astype(BF16)
    pieces = [
        lax.dynamic_index_in_dim(part, (y + step) % SIDE, 0, keepdims=False)
        for step in range(SIDE)
    ]
    return pieces[:1] + [
        lax.ppermute(pieces[step], "ctx", along_y(step)) for step in (1, 2, 3)
    ]


def stacked(ref):
    return ref[...].reshape(ref.shape[0] * ref.shape[1], ref.shape[2])


def square_sums(rows_ref, like):
    total = None
    for start in range(0, rows_ref.shape[1], like.shape[1]):
        part = rows_ref[:, start : start + like.shape[1]].astype(F32)
        total = part * part if total is None else total + part * part
    return jnp.broadcast_to(jnp.sum(total, axis=1, keepdims=True), like.shape)


def open_kernel(core, rows_ref, wg_ref, wu_ref, ag_ref, au_ref, ss_ref):
    ag_ref[...] = dot(rows_ref[...], stacked(wg_ref))
    au_ref[...] = dot(rows_ref[...], stacked(wu_ref))
    ss_ref[...] = square_sums(rows_ref, ss_ref)


def close_kernel(
    core, rows_ref, wg_ref, wu_ref, ag_in, au_in, ss_in, ga_ref,
    hact_ref, dg_ref, du_ref, dgi_ref, dui_ref, sc_ref,
):
    width = 2 * rows_ref.shape[1]
    total = (ss_in[...] + square_sums(rows_ref, ss_in))[:, :1]
    inv = lax.rsqrt(total / width + EPS)
    act_gate = inv * (ag_in[...] + dot(rows_ref[...], stacked(wg_ref)))
    act_up = inv * (au_in[...] + dot(rows_ref[...], stacked(wu_ref)))
    grad_act = ga_ref[...]
    sig = jax.nn.sigmoid(act_gate)
    swish = act_gate * sig
    slope = sig * (1.0 + act_gate * (1.0 - sig))
    hact = (swish * act_up).astype(BF16)
    dg32 = grad_act * act_up * slope
    du32 = grad_act * swish
    dg = dg32.astype(BF16)
    du = du32.astype(BF16)
    hact_ref[...] = hact
    dg_ref[...] = dg
    du_ref[...] = du
    dgi_ref[...] = (inv * dg32).astype(BF16)
    dui_ref[...] = (inv * du32).astype(BF16)
    probs = jnp.sum(hact.astype(F32) * grad_act, axis=1, keepdims=True)
    inner = jnp.sum(dg.astype(F32) * act_gate + du.astype(F32) * act_up, axis=1, keepdims=True)
    lane = lax.broadcasted_iota(jnp.int32, sc_ref.shape, 1)
    sc_ref[...] = jnp.where(
        lane == 0, probs, jnp.where(lane == 1, inner, jnp.where(lane == 2, inv, 0.0))
    )


def cot_kernel(core, own_ref, oth_ref, w_own_ref, w_oth_ref, ga_ref):
    ga_ref[...] = dot(own_ref[...], stacked(w_own_ref)) + dot(oth_ref[...], stacked(w_oth_ref))


def back_term(dg_ref, du_ref, wg_ref, wu_ref, block):
    return dot(dg_ref[...], wg_ref[block], ((1,), (1,))) + dot(
        du_ref[...], wu_ref[block], ((1,), (1,))
    )


def back_kernel(core, dg_ref, du_ref, wg_ref, wu_ref, out_ref):
    feat = wg_ref.shape[1]
    for block in range(wg_ref.shape[0]):
        term = back_term(dg_ref, du_ref, wg_ref, wu_ref, block)
        out_ref[:, block * feat : (block + 1) * feat] = term.astype(BF16)


def back_add(dg_ref, du_ref, wg_ref, wu_ref, other_ref, out_ref):
    feat = wg_ref.shape[1]
    for block in range(wg_ref.shape[0]):
        lanes = slice(block * feat, (block + 1) * feat)
        term = back_term(dg_ref, du_ref, wg_ref, wu_ref, block).astype(BF16).astype(F32)
        out_ref[:, lanes] = (term + other_ref[:, lanes].astype(F32)).astype(BF16)


def back_high_kernel(core, dg_ref, du_ref, wg_ref, wu_ref, other_ref, out_ref):
    back_add(dg_ref, du_ref, wg_ref, wu_ref, other_ref, out_ref)


def back_low_kernel(
    ctx_count, core, dg_ref, du_ref, wg_ref, wu_ref, other_ref, sc_ref, sc_other_ref, out_ref
):
    back_add(dg_ref, du_ref, wg_ref, wu_ref, other_ref, out_ref)
    small = sc_ref[...] + sc_other_ref[...]
    lane = lax.broadcasted_iota(jnp.int32, small.shape, 1)
    small = jnp.where(lane == 2, small * (0.5 / ctx_count), small)
    head = small.astype(BF16).astype(F32)
    tail = pltpu.roll(small - head, 3, 1)
    small = jnp.where(lane < 3, head, jnp.where(lane < 6, tail, 0.0))
    out_ref[:, other_ref.shape[1] :] = small.astype(BF16)


def scaled_grads_kernel(
    core, own_ref, oth_ref, gown_ref, goth_ref, dgi_ref, dui_ref, gate_ref, up_ref
):
    here = core[0]
    for rows_ref, gain_ref, place in ((own_ref, gown_ref, here), (oth_ref, goth_ref, 1 - here)):
        scaled = (rows_ref[...].astype(F32) * gain_ref[...]).astype(BF16)
        gate_ref[place] = dot(scaled, dgi_ref[...], ((0,), (0,))).astype(BF16)
        up_ref[place] = dot(scaled, dui_ref[...], ((0,), (0,))).astype(BF16)


def plain_grads_kernel(core, own_ref, oth_ref, act_ref, out_ref):
    here = core[0]
    out_ref[here] = dot(own_ref[...], act_ref[...], ((0,), (0,))).astype(BF16)
    out_ref[1 - here] = dot(oth_ref[...], act_ref[...], ((0,), (0,))).astype(BF16)


def sums_kernel(low_ref, h0_ref, h1_ref, h2_ref, h3_ref, out_ref):
    feat = out_ref.shape[2] - 128
    count = out_ref.shape[0] // 2

    def total(start, width):
        acc = low_ref[0, :, start : start + width].astype(F32)
        for block in range(1, low_ref.shape[0]):
            acc += low_ref[block, :, start : start + width].astype(F32)
        return acc

    small = total(count * feat, 128)
    lane = lax.broadcasted_iota(jnp.int32, small.shape, 1)
    small = jnp.where(lane < 3, small + pltpu.roll(small, 125, 1), 0.0)
    head = small.astype(BF16).astype(F32)
    small = (head + pltpu.roll(small - head, 3, 1)).astype(BF16)
    for block in range(count):
        out_ref[block, :, :feat] = total(block * feat, feat).astype(BF16)
        out_ref[block, :, feat:] = small
        lanes = slice(block * feat, (block + 1) * feat)
        high = h0_ref[:, lanes].astype(F32)
        for ref in (h1_ref, h2_ref, h3_ref):
            high += ref[:, lanes].astype(F32)
        out_ref[count + block, :, :feat] = high.astype(BF16)
        out_ref[count + block, :, feat:] = small


def whole(shape):
    return pl.BlockSpec(shape, lambda e, *_: (0,) * len(shape))


def side_by_side(blocks):
    return jnp.concatenate([blocks[e] for e in range(blocks.shape[0])], axis=1)


def per_device(
    residual,
    ssm_values,
    ssm_keys,
    ssm_queries,
    log_decay,
    expert_ids,
    gate_probs,
    norm_gain,
    w_gate,
    w_up,
    w_down,
    out_grad,
):
    tokens, feat = residual.shape
    heads = log_decay.shape[1]
    model_width, units = w_gate.shape[1:]
    ctx_count = lax.axis_size("ctx")
    exp_count = lax.axis_size("exp")
    capacity = 5 * tokens // (2 * exp_count)
    rows_all = ctx_count * capacity
    ctx_here = lax.axis_index("ctx")
    core = lax.axis_index("dp").astype(jnp.int32).reshape(1)
    other_core = [(0, 1), (1, 0)]

    values = ssm_values.astype(F32)
    key_rows = ssm_keys.astype(F32)
    queries = ssm_queries.astype(F32)
    (total_log, state_local), state_pull = jax.vjp(block_state, values, key_rows, log_decay)
    state_rows = state_local.shape[0]
    payload = jnp.concatenate(
        [state_local.astype(BF16), pad_rows(split_rows(total_log, 3), 8, feat)], axis=0
    )
    got = to_all(payload, "ctx")
    logs = jnp.sum(got[:, state_rows : state_rows + 3, :heads].astype(F32), axis=1)
    source = lax.broadcasted_iota(jnp.int32, (ctx_count, ctx_count), 0)
    between = lax.broadcasted_iota(jnp.int32, (ctx_count, ctx_count), 1)
    spread = head_map(heads, feat)
    rank = jnp.arange(ctx_count, dtype=jnp.int32)[:, None]
    before = ((between > source) & (between < ctx_here)).astype(F32)
    after = ((between < source) & (between > ctx_here)).astype(F32)
    gap_before = jnp.sum(before[:, :, None] * logs[None], axis=1)
    gap_after = jnp.sum(after[:, :, None] * logs[None], axis=1)
    weight_before = dot(
        jnp.where(rank < ctx_here, jnp.exp(gap_before), 0.0), spread, precision=HIGH
    )
    weight_after = dot(jnp.where(rank > ctx_here, jnp.exp(gap_after), 0.0), spread, precision=HIGH)
    state_in = jnp.sum(weight_before[:, None, :] * got[:, :state_rows].astype(F32), axis=0)

    ids = expert_ids.T
    probs = gate_probs.T
    experts = jnp.arange(exp_count, dtype=jnp.int32)[:, None]
    named = [ids[k][None, :] == experts for k in range(2)]
    member = named[0] | named[1]
    strict = (~lower_mask(tokens)).astype(BF16)
    order = dot(member.astype(BF16), strict).astype(jnp.int32)
    slot = lax.broadcasted_iota(jnp.int32, (exp_count, capacity, tokens), 1)
    chosen = (order[:, None, :] == slot) & member[:, None, :]
    select = chosen.astype(BF16).reshape(exp_count * capacity, tokens)
    select_each = jnp.concatenate(
        [
            (chosen & named[k][:, None, :]).astype(BF16).reshape(exp_count * capacity, tokens)
            for k in range(2)
        ],
        axis=1,
    )
    prob_of = jnp.where(named[0], probs[0][None, :], jnp.where(named[1], probs[1][None, :], 0.0))
    prob_rows = jnp.sum(jnp.where(chosen, prob_of[:, None, :], 0.0), axis=2)

    cot = (dot(select, out_grad).reshape(exp_count, capacity, feat) * prob_rows[:, :, None]).astype(
        BF16
    )
    mixer_out, output_pull = jax.vjp(
        block_output, values, key_rows, queries, log_decay, state_in
    )
    hidden = (residual.astype(F32) + mixer_out).astype(BF16)
    hidden_f = hidden.astype(F32)
    rows = dot(select, hidden).astype(BF16).reshape(exp_count, capacity, feat)
    gain_rows = pad_rows(split_rows(norm_gain[None, :], 3), 8, feat)
    gain_rows = jnp.broadcast_to(gain_rows[None], (exp_count,) + gain_rows.shape)
    got_rows = swap(jnp.concatenate([rows, cot, gain_rows], axis=1), "exp")
    gain_own = jnp.sum(got_rows[:, 2 * capacity : 2 * capacity + 3].astype(F32), axis=1)
    gain_oth = lax.ppermute(gain_own, "dp", other_core)
    gain4 = jnp.where(
        core[0] == 0,
        jnp.stack([gain_own, gain_oth], axis=1),
        jnp.stack([gain_oth, gain_own], axis=1),
    )
    gate4 = w_gate.reshape(exp_count, 2, feat, units)
    up4 = w_up.reshape(exp_count, 2, feat, units)
    down4 = w_down.reshape(exp_count, 2, feat, units)
    gate_scaled = (gate4.astype(F32) * gain4[:, :, :, None]).astype(BF16)
    up_scaled = (up4.astype(F32) * gain4[:, :, :, None]).astype(BF16)
    wide = exp_count * feat
    rows_all = ctx_count * capacity
    own = gather_rows(side_by_side(got_rows[:, :capacity])).reshape(rows_all, wide)
    cot_own = gather_cot(side_by_side(got_rows[:, capacity : 2 * capacity])).reshape(
        rows_all, wide
    )
    oth = lax.ppermute(own, "dp", other_core)
    cot_oth = lax.ppermute(cot_own, "dp", other_core)

    split = 2
    part = rows_all // split
    rows_spec = pl.BlockSpec((part, wide), lambda i, *_: (i, 0))
    acts = pl.BlockSpec((part, units), lambda i, *_: (i, 0))
    sums = pl.BlockSpec((part, 128), lambda i, *_: (i, 0))
    w_own = pl.BlockSpec((exp_count, None, feat, units), lambda i, s: (0, s[0], 0, 0))
    w_oth = pl.BlockSpec((exp_count, None, feat, units), lambda i, s: (0, 1 - s[0], 0, 0))
    acts_f = jax.ShapeDtypeStruct((rows_all, units), F32)
    acts_b = jax.ShapeDtypeStruct((rows_all, units), BF16)
    sums_f = jax.ShapeDtypeStruct((rows_all, 128), F32)

    def grid_of(n_scalars, steps, in_specs, out_specs):
        return pltpu.PrefetchScalarGridSpec(
            num_scalar_prefetch=n_scalars,
            grid=(steps,),
            in_specs=in_specs,
            out_specs=out_specs,
        )

    grad_act = pl.pallas_call(
        cot_kernel,
        grid_spec=grid_of(1, split, [rows_spec, rows_spec, w_own, w_oth], acts),
        out_shape=acts_f,
        name="cot",
    )(core, cot_own, cot_oth, down4, down4)
    ag, au, ss = pl.pallas_call(
        open_kernel,
        grid_spec=grid_of(1, split, [rows_spec, w_own, w_own], [acts, acts, sums]),
        out_shape=[acts_f, acts_f, sums_f],
        name="open",
    )(core, own, gate_scaled, up_scaled)
    hact, dg, du, dgi, dui, scal = pl.pallas_call(
        close_kernel,
        grid_spec=grid_of(
            1,
            split,
            [rows_spec, w_oth, w_oth, acts, acts, sums, acts],
            [acts] * 5 + [sums],
        ),
        out_shape=[acts_b] * 5 + [sums_f],
        name="close",
    )(core, oth, gate_scaled, up_scaled, ag, au, ss, grad_act)
    scal_got = lax.ppermute(scal, "dp", other_core)
    narrow = wide // 2
    half_rows = pl.BlockSpec((part, narrow), lambda i, *_: (i, 0))
    half_shape = jax.ShapeDtypeStruct((rows_all, narrow), BF16)
    half_w = (exp_count // 2, None, feat, units)
    near = [pl.BlockSpec(half_w, lambda i, s, k=k: (k, s[0], 0, 0)) for k in range(2)]
    far = [pl.BlockSpec(half_w, lambda i, s, k=k: (k, 1 - s[0], 0, 0)) for k in range(2)]
    swapped = []
    for k in range(2):
        sent = pl.pallas_call(
            back_kernel,
            grid_spec=grid_of(1, split, [acts, acts, far[k], far[k]], half_rows),
            out_shape=half_shape,
        )(core, dg, du, gate4, up4)
        swapped.append(lax.ppermute(sent, "dp", other_core))
    low = pl.pallas_call(
        functools.partial(back_low_kernel, ctx_count),
        grid_spec=grid_of(
            1,
            split,
            [acts, acts, near[0], near[0], half_rows, sums, sums],
            pl.BlockSpec((part, narrow + 128), lambda i, *_: (i, 0)),
        ),
        out_shape=jax.ShapeDtypeStruct((rows_all, narrow + 128), BF16),
        name="own_low",
    )(core, dg, du, gate4, up4, swapped[0], scal, scal_got)
    high = pl.pallas_call(
        back_high_kernel,
        grid_spec=grid_of(1, split, [acts, acts, near[1], near[1], half_rows], half_rows),
        out_shape=half_shape,
        name="own_high",
    )(core, dg, du, gate4, up4, swapped[1])
    columns = pl.BlockSpec((rows_all, feat), lambda e, *_: (0, e))
    gain_spec = pl.BlockSpec((None, 1, feat), lambda e, *_: (e, 0, 0))
    w_pair = pl.BlockSpec((None, 2, feat, units), lambda e, *_: (e, 0, 0, 0))
    acts_all = whole((rows_all, units))
    grads_shape = jax.ShapeDtypeStruct(gate4.shape, BF16)

    gate_grad, up_grad = pl.pallas_call(
        scaled_grads_kernel,
        grid_spec=grid_of(
            1,
            exp_count,
            [columns, columns, gain_spec, gain_spec, acts_all, acts_all],
            [w_pair] * 2,
        ),
        out_shape=[grads_shape] * 2,
        name="gate_grads",
    )(core, own, oth, gain_own[:, None], gain_oth[:, None], dgi, dui)
    down_grad = pl.pallas_call(
        plain_grads_kernel,
        grid_spec=grid_of(1, exp_count, [columns, columns, acts_all], w_pair),
        out_shape=grads_shape,
        name="down_grads",
    )(core, cot_own, cot_oth, hact)

    low = sum_low(low.reshape(SIDE, SIDE, capacity, narrow + 128))
    high = sum_high(high.reshape(SIDE, SIDE, capacity, narrow))
    summed = pl.pallas_call(
        sums_kernel,
        out_shape=jax.ShapeDtypeStruct((exp_count, capacity, feat + 128), BF16),
        name="sums",
    )(low, *high)
    got_back = swap(summed, "exp")
    got_back = got_back.reshape(exp_count * capacity, feat + 128)
    grad_normed = dot(select, got_back[:, :feat], ((0,), (0,)))
    small = dot(select_each, got_back[:, feat:], ((0,), (0,)))
    small = small[:, :3] + small[:, 3:6]
    grad_probs = (
        jnp.concatenate([small[:tokens, :1], small[tokens:, :1]], axis=1) / gate_probs
    )
    inner = small[:tokens, 1:2] + small[tokens:, 1:2]
    inv_rms = small[:tokens, 2:3]
    scaled = grad_normed * norm_gain[None, :]
    grad_hidden = (
        out_grad.astype(F32)
        + inv_rms * scaled
        - hidden_f * (inv_rms * inv_rms * inner / model_width)
    )
    gain_part = jnp.sum(grad_normed * hidden_f * inv_rms, axis=0, keepdims=True)

    vals_first, keys_first, queries_part, decay_first, carry_cot = output_pull(grad_hidden)
    got_carry = to_all(
        jnp.concatenate(
            [carry_cot.astype(BF16), pad_rows(split_rows(gain_part, 3), 8, feat)], axis=0
        ),
        "ctx",
    )
    grad_state = jnp.sum(weight_after[:, None, :] * got_carry[:, :state_rows].astype(F32), axis=0)
    grad_gain = jnp.sum(got_carry[:, state_rows : state_rows + 3].astype(F32), axis=(0, 1))
    grad_total = dot(
        jnp.sum(grad_state * state_in, axis=0, keepdims=True), spread, ((1,), (1,)), HIGH
    ) * jnp.exp(total_log)
    vals_second, keys_second, decay_second = state_pull((grad_total, grad_state))
    both = jnp.concatenate([keys_first + keys_second, queries_part], axis=1).astype(BF16)
    both = (both.astype(F32) + lax.ppermute(both, "dp", other_core).astype(F32)).astype(BF16)
    both = to_all(both, "exp")
    keys_grad = jnp.sum(both[:, :, :state_rows].astype(F32), axis=0)
    queries_grad = jnp.sum(both[:, :, state_rows:].astype(F32), axis=0)
    return (
        grad_hidden.astype(BF16),
        (vals_first + vals_second).astype(BF16),
        keys_grad,
        queries_grad,
        decay_first + decay_second,
        grad_probs,
        grad_gain,
        gate_grad.reshape(w_gate.shape),
        up_grad.reshape(w_up.shape),
        down_grad.reshape(w_down.shape),
    )


def solution(mesh):
    rows = P("ctx", ("exp", "dp"))
    weights = P("exp", None, ("ctx", "dp"))
    ctx = P("ctx", None)
    gain = P(("exp", "dp"))
    return jax.shard_map(
        per_device,
        mesh=mesh,
        in_specs=(
            rows, rows, ctx, ctx, rows, ctx, ctx, gain, weights, weights, weights, rows,
        ),
        out_specs=(rows, rows, ctx, ctx, rows, ctx, gain, weights, weights, weights),
        check_vma=False,
    )
```
